32 devices in a mesh: groups: 2 (over y), seq: 4 (over z), dp: 2 (over x), mp: 2 (over core).
Axes of the slice: x: 2, y: 2, z: 4, core: 2. Of those that a mesh axis runs over, the one named last changes fastest.
Arguments:
- queries: bfloat16 [4, 512, 2048], P(('groups', 'dp'), 'seq', 'mp'), parts along dimension 0, may hold values from -6 to 6
- keys: bfloat16 [4, 512, 2048], P(('groups', 'dp'), 'seq', 'mp'), parts along dimension 0, may hold values from -6 to 6
- values: bfloat16 [4, 512, 2048], P(('groups', 'dp'), 'seq', 'mp'), parts along dimension 0, may hold values from -6 to 6
- grad_output: bfloat16 [4, 512, 2048], P(('groups', 'dp'), 'seq', 'mp'), parts along dimension 0, may hold values from -6 to 6
- counts: int32 [4, 4, 4], P(('groups', 'dp'), 'seq'), parts along dimension 0, may hold values from 0 to 64, as said below
Outputs:
- grad_queries: bfloat16 [4, 512, 2048], P(('groups', 'dp'), 'seq', 'mp'), parts along dimension 0
- grad_keys: bfloat16 [4, 512, 2048], P(('groups', 'dp'), 'seq', 'mp'), parts along dimension 0
- grad_values: bfloat16 [4, 512, 2048], P(('groups', 'dp'), 'seq', 'mp'), parts along dimension 0
The draws below stay inside these ranges and needn't reach their ends.
There are 2 independent parts, one for each index of `groups`. The reference program is written for one: setup_inputs(seed, part) draws one part's arguments, and reference() takes and returns one part's arrays. A program takes and returns all parts, laid end to end along the dimension named above; each array names one. Nothing has to cross between parts.
Inputs may be any that keep to these rules, and one draw needn't show every extreme that they name: Each shard's counts sum to 128; no entry exceeds 64, some window receives 64 points from every shard.
All inputs are finite; a program needn't handle non-finite values.
Results may differ from the reference program's by a relative error of at most 0.001.
Values may be sent and summed in bfloat16 or wider, within the bound.
A program may use at most 128 MiB of HBM per device.

```python
import math
import jax
import jax.numpy as jnp
from jax import lax

HEADS = 16
DH = 128
R_SRC = 128
WIDTH = 2048
SLOT = 64
ROWS = 512
STREAMS = 2
N_SEQ = 4


def draw_counts(key, part):
    mean_count = R_SRC // N_SEQ
    half_seq = N_SEQ // 2
    first_key, second_key, third_key = jax.random.split(jax.random.fold_in(key, 7), 3)
    base = jax.random.randint(first_key, (STREAMS, 1, half_seq), 0, 2 * mean_count + 1)
    spread = jax.random.randint(second_key, (STREAMS, N_SEQ, half_seq), -(mean_count // 2), mean_count // 2 + 1)
    forced = jax.random.randint(third_key, (STREAMS, 1, 1), 0, half_seq)
    pair_index = jnp.arange(half_seq, dtype=jnp.int32)[None, None, :]
    first_half = jnp.clip(base + spread, 0, 2 * mean_count)
    first_half = jnp.where(pair_index == forced, 2 * mean_count, first_half)
    paired = jnp.stack([first_half, 2 * mean_count - first_half], axis=-1)
    return paired.reshape(STREAMS, N_SEQ, N_SEQ).astype(jnp.int32)


def level_of(rng, extent, cuts, least, top_value):
    level, own = 1.0, jax.random.fold_in(rng, 6)
    for dim, parts in cuts:
        steps = jnp.exp(jax.random.uniform(jax.random.fold_in(own, dim), (parts,), jnp.float32, least / len(cuts), top_value / len(cuts)))
        level = level * jnp.repeat(steps, extent[dim] // parts).reshape([-1 if axis == dim else 1 for axis in range(len(extent))])
    return level


def bell_draw(rng, dims, scale, limit, shards=(), held_as=jnp.bfloat16):
    drawn = scale * jax.random.normal(rng, dims, jnp.float32)
    if shards:
        drawn = drawn * level_of(rng, dims, shards, -0.22, 0.18)
    return jnp.clip(drawn, -limit, limit).astype(held_as)


def setup_inputs(seed: int = 0, part: int = 0) -> dict:
    key_of = jax.random.split(jax.random.key(seed), 6)
    part_keys = jax.random.split(jax.random.fold_in(key_of[5], part), 6)
    queries = bell_draw(part_keys[0], (STREAMS, ROWS, WIDTH), 1.0, 6.0, ((0, 2), (1, 4), (2, 2)))
    keys = bell_draw(part_keys[1], (STREAMS, ROWS, WIDTH), 1.0, 6.0, ((0, 2), (1, 4), (2, 2)))
    values = bell_draw(part_keys[2], (STREAMS, ROWS, WIDTH), 1.0, 6.0, ((0, 2), (1, 4), (2, 2)))
    grad_output = bell_draw(part_keys[3], (STREAMS, ROWS, WIDTH), 1.0, 6.0, ((0, 2), (1, 4), (2, 2)))
    counts = draw_counts(jax.random.fold_in(jax.random.fold_in(key_of[5], part), 71), part)
    return dict(queries=queries, keys=keys, values=values, grad_output=grad_output, counts=counts)


highest = lax.Precision.HIGHEST

def window_index(stream_counts):
    shard_starts = jnp.cumsum(stream_counts, axis=1) - stream_counts
    slot_offsets = jnp.arange(SLOT, dtype=jnp.int32)
    shard_base = jnp.arange(N_SEQ, dtype=jnp.int32) * R_SRC
    source_rows = shard_base[None, :, None] + shard_starts.T[:, :, None] + slot_offsets[None, None, :]
    occupied = slot_offsets[None, None, :] < stream_counts.T[:, :, None]
    return (source_rows.reshape(-1).astype(jnp.int32), occupied.reshape(-1))

def head_gradients(query_seq, key_seq, value_seq, grad_seq):
    total = query_seq.shape[0]
    block = 128 if total % 128 == 0 else total
    nblocks = total // block
    lower = (lax.broadcasted_iota(jnp.int32, (block, block), 0) >= lax.broadcasted_iota(jnp.int32, (block, block), 1)).astype(jnp.float32)
    pieces = tuple((x.reshape(nblocks, block, DH) for x in (query_seq, key_seq, value_seq, grad_seq)))

    def forward_step(state, part):
        query_b, key_b, value_b, grad_b = part
        weights = jnp.dot(grad_b, value_b.T, precision=highest) * lower
        grad_q = jnp.dot(grad_b, state.T, precision=highest) + jnp.dot(weights, key_b, precision=highest)
        state = state + jnp.dot(key_b.T, value_b, precision=highest)
        return (state, grad_q)

    def reverse_step(state, part):
        query_b, key_b, value_b, grad_b = part
        weights = jnp.dot(grad_b, value_b.T, precision=highest) * lower
        scores = jnp.dot(query_b, key_b.T, precision=highest) * lower
        grad_k = jnp.dot(value_b, state.T, precision=highest) + jnp.dot(weights.T, query_b, precision=highest)
        grad_v = jnp.dot(key_b, state, precision=highest) + jnp.dot(scores.T, grad_b, precision=highest)
        state = state + jnp.dot(query_b.T, grad_b, precision=highest)
        return (state, (grad_k, grad_v))
    start = jnp.zeros((DH, DH), jnp.float32)
    _, grad_q = lax.scan(forward_step, start, pieces)
    _, (grad_k, grad_v) = lax.scan(reverse_step, start, pieces, reverse=True)
    return (grad_q.reshape(total, DH), grad_k.reshape(total, DH), grad_v.reshape(total, DH))

def stream_gradients(operands):
    query_rows, key_rows, value_rows, grad_rows, stream_counts = operands
    factor = 1.0 / math.sqrt(DH * ROWS)
    source_rows, occupied = window_index(stream_counts)
    picked = jnp.where(occupied, source_rows, 0).astype(jnp.int32)

    def arrange(source):
        gathered = jnp.take(source, picked, axis=0).astype(jnp.float32)
        gathered = jnp.where(occupied[:, None], gathered, jnp.zeros_like(gathered))
        return gathered.reshape(-1, HEADS, DH).transpose(1, 0, 2)
    grad_q, grad_k, grad_v = jax.vmap(head_gradients)(arrange(query_rows), arrange(key_rows), arrange(value_rows), arrange(grad_rows))
    target = jnp.where(occupied, source_rows, ROWS).astype(jnp.int32)

    def place(result):
        flat_result = (result.transpose(1, 0, 2).reshape(-1, HEADS * DH) * factor).astype(jnp.bfloat16)
        return jnp.zeros((ROWS, HEADS * DH), jnp.bfloat16).at[target].set(flat_result, mode='drop')
    return (place(grad_q), place(grad_k), place(grad_v))

def reference(queries, keys, values, grad_output, counts):
    grad_queries, grad_keys, grad_values = lax.map(stream_gradients, (queries, keys, values, grad_output, counts))
    return (grad_queries, grad_keys, grad_values)
```

```python
import functools
import math

import jax
import jax.numpy as jnp
from jax import lax
from jax.experimental import pallas as pl
from jax.experimental.pallas import tpu as pltpu
from jax.sharding import PartitionSpec as P

DH = 128


highest = lax.Precision.HIGHEST


def entering(value, axis, join, neutral, backward):
    count, mine = (lax.axis_size(axis), lax.axis_index(axis))
    pieces = lax.all_gather(value, axis)
    if backward:
        pieces = pieces[::-1]
        mine = count - 1 - mine
    total = jnp.full_like(value, 0) + jnp.asarray(neutral, value.dtype)

    def hop(position, total):
        longer = join(total, pieces[position])
        return jnp.where(position < mine, longer, total)

    return lax.fori_loop(0, count - 1, hop, total)


def add_states(earlier, later):
    return earlier + later


def per_device(queries, keys, values, grad_output, counts):
    shard_count = lax.axis_size("seq")
    local_rows = queries.shape[1]
    width = queries.shape[2]
    local_heads = width // DH
    capacity = 2 * local_rows // shard_count
    window_rows = shard_count * capacity
    factor = 1.0 / math.sqrt(DH * local_rows * shard_count)
    my_counts = counts[0, 0]
    upto = jnp.arange(shard_count)[:, None] >= jnp.arange(shard_count)[None, :]
    window_ends = jnp.sum(jnp.where(upto, my_counts[None, :], 0), axis=1)
    window_starts = window_ends - my_counts
    offsets = jnp.arange(capacity, dtype=jnp.int32)
    occupied = offsets[None, :] < my_counts[:, None]
    picked = jnp.where(occupied, window_starts[:, None] + offsets[None, :], 0).reshape(-1)
    occupied_column = occupied.reshape(-1, 1)

    def pack(source):
        taken = jnp.take(source[0], picked, axis=0)
        taken = jnp.where(occupied_column, taken, jnp.zeros_like(taken))
        return taken.reshape(shard_count, capacity, width)

    def split_heads(received):
        return received.reshape(window_rows, local_heads, DH)

    def outer_sum(left, right):
        return jnp.einsum("lha,lhb->hab", left, right, preferred_element_type=jnp.float32)

    query_recv, key_recv, value_recv, grad_recv = (
        lax.all_to_all(pack(queries), "seq", split_axis=0, concat_axis=0, tiled=True),
        lax.all_to_all(pack(keys), "seq", split_axis=0, concat_axis=0, tiled=True),
        lax.all_to_all(pack(values), "seq", split_axis=0, concat_axis=0, tiled=True),
        lax.all_to_all(pack(grad_output), "seq", split_axis=0, concat_axis=0, tiled=True),
    )
    query_recv = split_heads(query_recv)
    key_recv = split_heads(key_recv)
    value_recv = split_heads(value_recv)
    grad_recv = split_heads(grad_recv)
    key_state = outer_sum(key_recv, value_recv)
    query_state = outer_sum(query_recv, grad_recv)
    zero_state = jnp.zeros((local_heads, DH, DH), jnp.float32)
    before_kv = entering(key_state, "seq", add_states, zero_state, False)
    after_qd = entering(query_state, "seq", add_states, zero_state, True)
    block = min(512, window_rows)
    nblocks = window_rows // block

    def blocked(received):
        return received.reshape(nblocks, block, local_heads, DH)

    query_blocks = blocked(query_recv)
    key_blocks = blocked(key_recv)
    value_blocks = blocked(value_recv)
    grad_blocks = blocked(grad_recv)
    block_kv = jnp.einsum(
        "nlha,nlhb->nhab", key_blocks, value_blocks, preferred_element_type=jnp.float32
    )
    block_qd = jnp.einsum(
        "nlha,nlhb->nhab", query_blocks, grad_blocks, preferred_element_type=jnp.float32
    )
    kv_before = before_kv[None] + jnp.cumsum(block_kv, axis=0) - block_kv
    qd_after = after_qd[None] + jnp.sum(block_qd, axis=0)[None] - jnp.cumsum(block_qd, axis=0)
    lower = (
        lax.broadcasted_iota(jnp.int32, (block, block), 0)
        >= lax.broadcasted_iota(jnp.int32, (block, block), 1)
    ).astype(jnp.float32)

    def one_block(pieces):
        query_part, key_part, value_part, grad_part, kv_state, qd_state = pieces
        weights = (
            jnp.einsum("rha,sha->hrs", grad_part, value_part, preferred_element_type=jnp.float32)
            * lower[None]
        )
        scores = (
            jnp.einsum("rha,sha->hrs", query_part, key_part, preferred_element_type=jnp.float32)
            * lower[None]
        )
        query_f = query_part.astype(jnp.float32)
        key_f = key_part.astype(jnp.float32)
        value_f = value_part.astype(jnp.float32)
        grad_f = grad_part.astype(jnp.float32)
        grad_q = jnp.einsum("rhb,hab->rha", grad_f, kv_state, precision=highest) + jnp.einsum(
            "hrs,sha->rha", weights, key_f, precision=highest
        )
        grad_k = jnp.einsum("shb,hab->sha", value_f, qd_state, precision=highest) + jnp.einsum(
            "hrs,rha->sha", weights, query_f, precision=highest
        )
        grad_v = jnp.einsum("sha,hab->shb", key_f, qd_state, precision=highest) + jnp.einsum(
            "hrs,rhb->shb", scores, grad_f, precision=highest
        )

        def finish(result):
            return (result * factor).astype(jnp.bfloat16).reshape(block, width)

        return (finish(grad_q), finish(grad_k), finish(grad_v))

    out_q, out_k, out_v = lax.map(
        one_block, (query_blocks, key_blocks, value_blocks, grad_blocks, kv_before, qd_after)
    )

    def to_slots(result):
        return result.reshape(shard_count, capacity, width)

    back_q, back_k, back_v = (
        lax.all_to_all(to_slots(out_q), "seq", split_axis=0, concat_axis=0, tiled=True),
        lax.all_to_all(to_slots(out_k), "seq", split_axis=0, concat_axis=0, tiled=True),
        lax.all_to_all(to_slots(out_v), "seq", split_axis=0, concat_axis=0, tiled=True),
    )
    positions = jnp.arange(local_rows, dtype=jnp.int32)
    member = (
        (positions[:, None] >= window_starts[None, :]) & (positions[:, None] < window_ends[None, :])
    ).astype(jnp.int32)
    window_of = jnp.sum(member * jnp.arange(shard_count, dtype=jnp.int32)[None, :], axis=1)
    start_of = jnp.sum(member * window_starts[None, :], axis=1)
    source_index = window_of * capacity + positions - start_of

    def unpack(returned):
        return jnp.take(returned.reshape(window_rows, width), source_index, axis=0)[None]

    return (unpack(back_q), unpack(back_k), unpack(back_v))


MESH = pl.DeviceIdType.MESH
VMEM_LIMIT = 16 << 20


AHEAD = 4
LAG = 4


def line_kernel(
    rows,
    heads,
    q_ref,
    k_ref,
    v_ref,
    g_ref,
    counts_ref,
    grads_ref,
    qg,
    kv,
    mine,
    ends,
    key_row,
    key_col,
    near,
    grad_out,
    part_out,
    part_in,
    scale_out,
    scale_in,
    mine_sem,
    own_sem,
    ends_send,
    ends_recv,
    qg_send,
    qg_recv,
    kv_send,
    kv_recv,
    pair_send,
    pair_recv,
    dq_send,
    dq_recv,
    part_send,
    part_recv,
    scale_send,
    scale_recv,
):
    n = 4
    me = lax.axis_index("seq")
    factor = 1.0 / math.sqrt(DH * n * rows)
    side = me // 2
    partner = me + 1 - 2 * lax.rem(me, 2)
    opp = n - 1 - me
    cross = n - 1 - partner
    is_inner = jnp.logical_or(me == 1, me == 2)
    is_outer = jnp.logical_not(is_inner)

    def columns(head):
        return pl.ds(pl.multiple_of(head * DH, DH), DH)

    def block(shard):
        return pl.ds(pl.multiple_of(shard * rows, rows), rows)

    def half(shard):
        return block(lax.rem(shard, 2))

    def remote(source, target, send, recv, device):
        return pltpu.make_async_remote_copy(
            src_ref=source,
            dst_ref=target,
            send_sem=send,
            recv_sem=recv,
            device_id={"seq": device},
            device_id_type=MESH,
        )

    barrier = pltpu.get_barrier_semaphore()
    pl.semaphore_signal(barrier, inc=1, device_id={"seq": partner}, device_id_type=MESH)

    @pl.when(is_inner)
    def _():
        pl.semaphore_signal(barrier, inc=1, device_id={"seq": opp}, device_id_type=MESH)

    load = pltpu.make_async_copy(counts_ref, mine, mine_sem)
    load.start()

    def own_copy(h, i):
        source = (g_ref, q_ref, k_ref, v_ref)[i].at[0, :, columns(h)]
        target = qg.at[h, i, block(me)] if i < 2 else kv.at[h, i - 2, half(me)]
        return pltpu.make_async_copy(source, target, own_sem.at[h, i])

    @pl.loop(0, heads)
    def _(h):
        for i in range(4):
            own_copy(h, i).start()

    load.wait()
    lanes = lax.broadcasted_iota(jnp.int32, (8, 128), 1)
    end = jnp.zeros((1, 1), jnp.int32)
    table = jnp.zeros((8, 128), jnp.int32)
    for w in range(n):
        end = end + mine[0, 0:1, w : w + 1]
        table = jnp.where(lanes == w, end, table)
    ends[me] = table

    pl.semaphore_wait(barrier, jnp.where(is_inner, 2, 1))

    def ends_copy(shard, which, device):
        return remote(ends.at[shard], ends.at[shard], ends_send.at[which], ends_recv.at[which], device)

    def qg_copy(h, shard, which, device):
        at = qg.at[h, :, block(shard)]
        return remote(at, at, qg_send.at[h, which], qg_recv.at[h, which], device)

    def kv_copy(h, shard):
        at = kv.at[h, :, half(shard)]
        return remote(at, at, kv_send.at[h], kv_recv.at[h], partner)

    @pl.when(is_outer)
    def _():
        ends_copy(me, 0, partner).start()

        def give_qg(h):
            own_copy(h, 0).wait()
            own_copy(h, 1).wait()
            qg_copy(h, me, 0, partner).start()

        def give_kv(h):
            own_copy(h, 2).wait()
            own_copy(h, 3).wait()
            kv_copy(h, me).start()

        give_qg(0)

        @pl.loop(0, heads)
        def _(h):
            give_kv(h)
            for later in (2 * h + 1, 2 * h + 2):

                @pl.when(later < heads)
                def _():
                    give_qg(later)

    def scores(left, right):
        return lax.dot_general(
            left, right, (((1,), (1,)), ((), ())), preferred_element_type=jnp.float32
        )

    def weighted(weights, right):
        high = weights.astype(jnp.bfloat16)
        low = (weights - high.astype(jnp.float32)).astype(jnp.bfloat16)
        product = jnp.dot(high, right, preferred_element_type=jnp.float32) + jnp.dot(
            low, right, preferred_element_type=jnp.float32
        )
        return product * factor

    def masked(weights, shard, others, forward):
        col = key_col[shard]
        pieces = []
        for i, other in enumerate(others):
            row = key_row[other][0:1, :]
            keep = (row <= col) if forward else (row >= col)
            pieces.append(jnp.where(keep, weights[:, i * rows : (i + 1) * rows], 0.0))
        return jnp.concatenate(pieces, axis=1)

    def part_copy(h):
        return remote(part_out.at[h], part_in.at[h], part_send.at[h], part_recv.at[h], opp)

    def scale_copy(h):
        return remote(scale_out.at[h], scale_in.at[h], scale_send.at[h], scale_recv.at[h], opp)

    def pair_copy(h, which):
        source, target = grad_out.at[h, which, pl.ds(1, 2)], grads_ref.at[h, pl.ds(1, 2)]
        if which == 1:
            return pltpu.make_async_copy(source, target, pair_send.at[h, 1])
        return remote(source, target, pair_send.at[h, 0], pair_recv.at[h], partner)

    def dq_copy(h, which):
        source, target = grad_out.at[h, which, 0], grads_ref.at[h, 0]
        if which == 1:
            return pltpu.make_async_copy(source, target, dq_send.at[h, 1])
        return remote(source, target, dq_send.at[h, 0], dq_recv.at[h], partner)

    @pl.when(is_inner)
    def _():
        ends_copy(me, 1, opp).start()

        def own_to_opp(h):
            own_copy(h, 0).wait()
            own_copy(h, 1).wait()
            qg_copy(h, me, 1, opp).start()

        @pl.loop(0, AHEAD)
        def _(h):
            own_to_opp(h)

        ends_copy(partner, 0, partner).wait_recv()
        ends_copy(partner, 2, opp).start()

        def relay(h):
            qg_copy(h, partner, 0, partner).wait_recv()
            qg_copy(h, partner, 2, opp).start()

        relay(0)

        @pl.loop(AHEAD, heads)
        def _(h):
            own_to_opp(h)

        ends_copy(opp, 1, opp).wait_recv()
        ends_copy(cross, 2, opp).wait_recv()

        across = lax.broadcasted_iota(jnp.int32, (8, rows), 1)
        down = lax.broadcasted_iota(jnp.int32, (rows, 128), 0)
        for s in range(n):
            window_row = jnp.zeros((8, rows), jnp.int32)
            window_col = jnp.zeros((rows, 128), jnp.int32)
            for w in range(n):
                stop = ends[s, 0:1, w : w + 1]
                window_row = window_row + jnp.where(across >= stop, 1, 0)
                window_col = window_col + jnp.where(down >= stop, 1, 0)
            key_row[s] = (window_row * n + s) * rows + across
            key_col[s] = (window_col * n + s) * rows + down

        def finish(h):
            part_copy(h).wait_recv()
            scale_copy(h).wait_recv()
            for which in range(2):
                far = part_in[h, which].astype(jnp.int32).astype(jnp.float32) * scale_in[h, which]
                grad_out[h, which, 0] = (near[h, which] + far).astype(jnp.bfloat16)
                dq_copy(h, which).start()

        @pl.loop(0, heads)
        def _(h):
            for later in (2 * h + 1, 2 * h + 2):

                @pl.when(later < heads)
                def _():
                    relay(later)

            own_copy(h, 2).wait()
            own_copy(h, 3).wait()
            kv_copy(h, partner).wait_recv()
            key_all = kv[h, 0]
            value_all = kv[h, 1]
            def part(shard):
                grad = qg[h, 0, block(shard), :]
                weights = masked(scores(grad, value_all), shard, (2 * side, 2 * side + 1), True)
                return weighted(weights, key_all)

            for which, shard in enumerate((cross, opp)):
                qg_copy(h, shard, 2 - which, opp).wait_recv()
            for which, shard in enumerate((cross, opp)):
                far = part(shard)
                top = jnp.maximum(jnp.max(jnp.abs(far), axis=0, keepdims=True), 1e-30)
                part_out[h, which] = jnp.round(far * (32767.0 / top)).astype(jnp.int32).astype(jnp.int16)
                scale_out[h, which] = top * (1.0 / 32767.0)
            part_copy(h).start()
            scale_copy(h).start()
            for which, shard in enumerate((partner, me)):
                near[h, which] = part(shard)
            grad_all = qg[h, 0]
            query_all = qg[h, 1]
            for which, shard in enumerate((partner, me)):
                key = kv[h, 0, half(shard), :]
                value = kv[h, 1, half(shard), :]
                shards = tuple(range(n))
                grad_out[h, which, 1] = weighted(
                    masked(scores(value, grad_all), shard, shards, False), query_all
                ).astype(jnp.bfloat16)
                grad_out[h, which, 2] = weighted(
                    masked(scores(key, query_all), shard, shards, False), grad_all
                ).astype(jnp.bfloat16)
                pair_copy(h, which).start()

            @pl.when(h >= LAG)
            def _():
                finish(h - LAG)

        @pl.loop(heads - LAG, heads)
        def _(h):
            finish(h)

        ends_copy(me, 1, opp).wait_send()
        ends_copy(partner, 2, opp).wait_send()

        @pl.loop(0, heads)
        def _(h):
            qg_copy(h, me, 1, opp).wait_send()
            qg_copy(h, partner, 2, opp).wait_send()
            pair_copy(h, 0).wait_send()
            pair_copy(h, 1).wait()
            part_copy(h).wait_send()
            scale_copy(h).wait_send()
            dq_copy(h, 0).wait_send()
            dq_copy(h, 1).wait()

    @pl.when(is_outer)
    def _():
        ends_copy(me, 0, partner).wait_send()

        @pl.loop(0, heads)
        def _(h):
            qg_copy(h, me, 0, partner).wait_send()
            kv_copy(h, me).wait_send()
            pair_copy(h, 0).wait_recv()
            dq_copy(h, 0).wait_recv()


def place_kernel(heads, grads_ref, dq_ref, dk_ref, dv_ref, sem):
    copies = [
        pltpu.make_async_copy(
            grads_ref.at[h, i], target.at[0, :, pl.ds(h * DH, DH)], sem.at[h, i]
        )
        for h in range(heads)
        for i, target in enumerate((dq_ref, dk_ref, dv_ref))
    ]
    for copy in copies:
        copy.start()
    for copy in copies:
        copy.wait()


def by_line(queries, keys, values, grad_output, counts):
    n = 4
    rows, width = queries.shape[1:]
    heads = width // DH
    dma = pltpu.SemaphoreType.DMA
    anywhere = pl.BlockSpec(memory_space=pl.ANY)
    packed = pl.pallas_call(
        functools.partial(line_kernel, rows, heads),
        out_shape=jax.ShapeDtypeStruct((heads, 3, rows, DH), jnp.bfloat16),
        in_specs=[pl.BlockSpec(memory_space=pltpu.HBM)] * 5,
        out_specs=anywhere,
        scratch_shapes=[
            pltpu.VMEM((heads, 2, n * rows, DH), jnp.bfloat16),
            pltpu.VMEM((heads, 2, 2 * rows, DH), jnp.bfloat16),
            pltpu.VMEM((1, 1, n), jnp.int32),
            pltpu.VMEM((n, 8, 128), jnp.int32),
            pltpu.VMEM((n, 8, rows), jnp.int32),
            pltpu.VMEM((n, rows, 128), jnp.int32),
            pltpu.VMEM((heads, 2, rows, DH), jnp.float32),
            pltpu.VMEM((heads, 2, 3, rows, DH), jnp.bfloat16),
            pltpu.VMEM((heads, 2, rows, DH), jnp.int16),
            pltpu.VMEM((heads, 2, rows, DH), jnp.int16),
            pltpu.VMEM((heads, 2, 1, DH), jnp.float32),
            pltpu.VMEM((heads, 2, 1, DH), jnp.float32),
            dma(()),
            dma((heads, 4)),
            dma((3,)),
            dma((3,)),
            dma((heads, 3)),
            dma((heads, 3)),
            dma((heads,)),
            dma((heads,)),
            dma((heads, 2)),
            dma((heads,)),
            dma((heads, 2)),
            dma((heads,)),
            dma((heads,)),
            dma((heads,)),
            dma((heads,)),
            dma((heads,)),
        ],
        compiler_params=pltpu.CompilerParams(collective_id=0, has_side_effects=True, vmem_limit_bytes=VMEM_LIMIT),
    )(*(pltpu.with_memory_space_constraint(x, pltpu.HBM) for x in (queries, keys, values, grad_output, counts)))
    return pl.pallas_call(
        functools.partial(place_kernel, heads),
        out_shape=[jax.ShapeDtypeStruct(queries.shape, jnp.bfloat16)] * 3,
        in_specs=[anywhere],
        out_specs=[anywhere] * 3,
        scratch_shapes=[dma((heads, 3))],
        compiler_params=pltpu.CompilerParams(vmem_limit_bytes=VMEM_LIMIT),
    )(packed)


def per_shard(queries, keys, values, grad_output, counts):
    n = lax.axis_size("seq")
    if n == 4 and queries.shape[1] == 128:
        return by_line(queries, keys, values, grad_output, counts)
    return per_device(queries, keys, values, grad_output, counts)


def solution(mesh):
    placed = (
        P(("groups", "dp"), "seq", "mp"),
        P(("groups", "dp"), "seq", "mp"),
        P(("groups", "dp"), "seq", "mp"),
        P(("groups", "dp"), "seq", "mp"),
        P(("groups", "dp"), "seq", None),
    )
    return jax.shard_map(
        per_shard,
        mesh=mesh,
        in_specs=placed,
        out_specs=(
            P(("groups", "dp"), "seq", "mp"),
            P(("groups", "dp"), "seq", "mp"),
            P(("groups", "dp"), "seq", "mp"),
        ),
        check_vma=False,
    )
```

```python
import functools
import math

import jax
import jax.numpy as jnp
from jax import lax
from jax.experimental import pallas as pl
from jax.experimental.pallas import tpu as pltpu
from jax.sharding import PartitionSpec as P

DH = 128


highest = lax.Precision.HIGHEST


def entering(value, axis, join, neutral, backward):
    count, mine = (lax.axis_size(axis), lax.axis_index(axis))
    pieces = lax.all_gather(value, axis)
    if backward:
        pieces = pieces[::-1]
        mine = count - 1 - mine
    total = jnp.full_like(value, 0) + jnp.asarray(neutral, value.dtype)

    def hop(position, total):
        longer = join(total, pieces[position])
        return jnp.where(position < mine, longer, total)

    return lax.fori_loop(0, count - 1, hop, total)


def add_states(earlier, later):
    return earlier + later


def per_device(queries, keys, values, grad_output, counts):
    shard_count = lax.axis_size("seq")
    local_rows = queries.shape[1]
    width = queries.shape[2]
    local_heads = width // DH
    capacity = 2 * local_rows // shard_count
    window_rows = shard_count * capacity
    factor = 1.0 / math.sqrt(DH * local_rows * shard_count)
    my_counts = counts[0, 0]
    upto = jnp.arange(shard_count)[:, None] >= jnp.arange(shard_count)[None, :]
    window_ends = jnp.sum(jnp.where(upto, my_counts[None, :], 0), axis=1)
    window_starts = window_ends - my_counts
    offsets = jnp.arange(capacity, dtype=jnp.int32)
    occupied = offsets[None, :] < my_counts[:, None]
    picked = jnp.where(occupied, window_starts[:, None] + offsets[None, :], 0).reshape(-1)
    occupied_column = occupied.reshape(-1, 1)

    def pack(source):
        taken = jnp.take(source[0], picked, axis=0)
        taken = jnp.where(occupied_column, taken, jnp.zeros_like(taken))
        return taken.reshape(shard_count, capacity, width)

    def split_heads(received):
        return received.reshape(window_rows, local_heads, DH)

    def outer_sum(left, right):
        return jnp.einsum("lha,lhb->hab", left, right, preferred_element_type=jnp.float32)

    query_recv, key_recv, value_recv, grad_recv = (
        lax.all_to_all(pack(queries), "seq", split_axis=0, concat_axis=0, tiled=True),
        lax.all_to_all(pack(keys), "seq", split_axis=0, concat_axis=0, tiled=True),
        lax.all_to_all(pack(values), "seq", split_axis=0, concat_axis=0, tiled=True),
        lax.all_to_all(pack(grad_output), "seq", split_axis=0, concat_axis=0, tiled=True),
    )
    query_recv = split_heads(query_recv)
    key_recv = split_heads(key_recv)
    value_recv = split_heads(value_recv)
    grad_recv = split_heads(grad_recv)
    key_state = outer_sum(key_recv, value_recv)
    query_state = outer_sum(query_recv, grad_recv)
    zero_state = jnp.zeros((local_heads, DH, DH), jnp.float32)
    before_kv = entering(key_state, "seq", add_states, zero_state, False)
    after_qd = entering(query_state, "seq", add_states, zero_state, True)
    block = min(512, window_rows)
    nblocks = window_rows // block

    def blocked(received):
        return received.reshape(nblocks, block, local_heads, DH)

    query_blocks = blocked(query_recv)
    key_blocks = blocked(key_recv)
    value_blocks = blocked(value_recv)
    grad_blocks = blocked(grad_recv)
    block_kv = jnp.einsum(
        "nlha,nlhb->nhab", key_blocks, value_blocks, preferred_element_type=jnp.float32
    )
    block_qd = jnp.einsum(
        "nlha,nlhb->nhab", query_blocks, grad_blocks, preferred_element_type=jnp.float32
    )
    kv_before = before_kv[None] + jnp.cumsum(block_kv, axis=0) - block_kv
    qd_after = after_qd[None] + jnp.sum(block_qd, axis=0)[None] - jnp.cumsum(block_qd, axis=0)
    lower = (
        lax.broadcasted_iota(jnp.int32, (block, block), 0)
        >= lax.broadcasted_iota(jnp.int32, (block, block), 1)
    ).astype(jnp.float32)

    def one_block(pieces):
        query_part, key_part, value_part, grad_part, kv_state, qd_state = pieces
        weights = (
            jnp.einsum("rha,sha->hrs", grad_part, value_part, preferred_element_type=jnp.float32)
            * lower[None]
        )
        scores = (
            jnp.einsum("rha,sha->hrs", query_part, key_part, preferred_element_type=jnp.float32)
            * lower[None]
        )
        query_f = query_part.astype(jnp.float32)
        key_f = key_part.astype(jnp.float32)
        value_f = value_part.astype(jnp.float32)
        grad_f = grad_part.astype(jnp.float32)
        grad_q = jnp.einsum("rhb,hab->rha", grad_f, kv_state, precision=highest) + jnp.einsum(
            "hrs,sha->rha", weights, key_f, precision=highest
        )
        grad_k = jnp.einsum("shb,hab->sha", value_f, qd_state, precision=highest) + jnp.einsum(
            "hrs,rha->sha", weights, query_f, precision=highest
        )
        grad_v = jnp.einsum("sha,hab->shb", key_f, qd_state, precision=highest) + jnp.einsum(
            "hrs,rhb->shb", scores, grad_f, precision=highest
        )

        def finish(result):
            return (result * factor).astype(jnp.bfloat16).reshape(block, width)

        return (finish(grad_q), finish(grad_k), finish(grad_v))

    out_q, out_k, out_v = lax.map(
        one_block, (query_blocks, key_blocks, value_blocks, grad_blocks, kv_before, qd_after)
    )

    def to_slots(result):
        return result.reshape(shard_count, capacity, width)

    back_q, back_k, back_v = (
        lax.all_to_all(to_slots(out_q), "seq", split_axis=0, concat_axis=0, tiled=True),
        lax.all_to_all(to_slots(out_k), "seq", split_axis=0, concat_axis=0, tiled=True),
        lax.all_to_all(to_slots(out_v), "seq", split_axis=0, concat_axis=0, tiled=True),
    )
    positions = jnp.arange(local_rows, dtype=jnp.int32)
    member = (
        (positions[:, None] >= window_starts[None, :]) & (positions[:, None] < window_ends[None, :])
    ).astype(jnp.int32)
    window_of = jnp.sum(member * jnp.arange(shard_count, dtype=jnp.int32)[None, :], axis=1)
    start_of = jnp.sum(member * window_starts[None, :], axis=1)
    source_index = window_of * capacity + positions - start_of

    def unpack(returned):
        return jnp.take(returned.reshape(window_rows, width), source_index, axis=0)[None]

    return (unpack(back_q), unpack(back_k), unpack(back_v))


MESH = pl.DeviceIdType.MESH
VMEM_LIMIT = 16 << 20


AHEAD = 4
LAG = 2


def line_kernel(
    rows,
    heads,
    q_ref,
    k_ref,
    v_ref,
    g_ref,
    counts_ref,
    grads_ref,
    qg,
    kv,
    mine,
    ends,
    key_row,
    key_col,
    near,
    grad_out,
    part_out,
    part_in,
    scale_out,
    scale_in,
    mine_sem,
    own_sem,
    ends_send,
    ends_recv,
    qg_send,
    qg_recv,
    kv_send,
    kv_recv,
    pair_send,
    pair_recv,
    dq_send,
    dq_recv,
    part_send,
    part_recv,
    scale_send,
    scale_recv,
):
    n = 4
    me = lax.axis_index("seq")
    factor = 1.0 / math.sqrt(DH * n * rows)
    side = me // 2
    partner = me + 1 - 2 * lax.rem(me, 2)
    opp = n - 1 - me
    cross = n - 1 - partner
    is_inner = jnp.logical_or(me == 1, me == 2)
    is_outer = jnp.logical_not(is_inner)

    def columns(head):
        return pl.ds(pl.multiple_of(head * DH, DH), DH)

    def block(shard):
        return pl.ds(pl.multiple_of(shard * rows, rows), rows)

    def half(shard):
        return block(lax.rem(shard, 2))

    def remote(source, target, send, recv, device):
        return pltpu.make_async_remote_copy(
            src_ref=source,
            dst_ref=target,
            send_sem=send,
            recv_sem=recv,
            device_id={"seq": device},
            device_id_type=MESH,
        )

    barrier = pltpu.get_barrier_semaphore()
    pl.semaphore_signal(barrier, inc=1, device_id={"seq": partner}, device_id_type=MESH)

    @pl.when(is_inner)
    def _():
        pl.semaphore_signal(barrier, inc=1, device_id={"seq": opp}, device_id_type=MESH)

    load = pltpu.make_async_copy(counts_ref, mine, mine_sem)
    load.start()

    def own_copy(h, i):
        source = (g_ref, q_ref, k_ref, v_ref)[i].at[0, :, columns(h)]
        target = qg.at[h, i, block(me)] if i < 2 else kv.at[h, i - 2, half(me)]
        return pltpu.make_async_copy(source, target, own_sem.at[h, i])

    @pl.loop(0, heads)
    def _(h):
        for i in range(4):
            own_copy(h, i).start()

    load.wait()
    lanes = lax.broadcasted_iota(jnp.int32, (8, 128), 1)
    end = jnp.zeros((1, 1), jnp.int32)
    table = jnp.zeros((8, 128), jnp.int32)
    for w in range(n):
        end = end + mine[0, 0:1, w : w + 1]
        table = jnp.where(lanes == w, end, table)
    ends[me] = table

    pl.semaphore_wait(barrier, jnp.where(is_inner, 2, 1))

    def ends_copy(shard, which, device):
        return remote(ends.at[shard], ends.at[shard], ends_send.at[which], ends_recv.at[which], device)

    def qg_copy(h, shard, which, device):
        at = qg.at[h, :, block(shard)]
        return remote(at, at, qg_send.at[h, which], qg_recv.at[h, which], device)

    def kv_copy(h, shard):
        at = kv.at[h, :, half(shard)]
        return remote(at, at, kv_send.at[h], kv_recv.at[h], partner)

    @pl.when(is_outer)
    def _():
        ends_copy(me, 0, partner).start()

        def give_qg(h):
            own_copy(h, 0).wait()
            own_copy(h, 1).wait()
            qg_copy(h, me, 0, partner).start()

        def give_kv(h):
            own_copy(h, 2).wait()
            own_copy(h, 3).wait()
            kv_copy(h, me).start()

        give_qg(0)

        @pl.loop(0, heads)
        def _(h):
            give_kv(h)
            for later in (2 * h + 1, 2 * h + 2):

                @pl.when(later < heads)
                def _():
                    give_qg(later)

    def scores(left, right):
        return lax.dot_general(
            left, right, (((1,), (1,)), ((), ())), preferred_element_type=jnp.float32
        )

    def weighted(weights, right):
        high = weights.astype(jnp.bfloat16)
        low = (weights - high.astype(jnp.float32)).astype(jnp.bfloat16)
        product = jnp.dot(high, right, preferred_element_type=jnp.float32) + jnp.dot(
            low, right, preferred_element_type=jnp.float32
        )
        return product * factor

    def masked(weights, shard, others, forward):
        col = key_col[shard]
        pieces = []
        for i, other in enumerate(others):
            row = key_row[other][0:1, :]
            keep = (row <= col) if forward else (row >= col)
            pieces.append(jnp.where(keep, weights[:, i * rows : (i + 1) * rows], 0.0))
        return jnp.concatenate(pieces, axis=1)

    def part_copy(h, which):
        return remote(
            part_out.at[h, which],
            part_in.at[h, which],
            part_send.at[h, which],
            part_recv.at[h, which],
            opp,
        )

    def scale_copy(h):
        return remote(scale_out.at[h], scale_in.at[h], scale_send.at[h], scale_recv.at[h], opp)

    def pair_copy(h, which):
        source, target = grad_out.at[h, which, pl.ds(1, 2)], grads_ref.at[h, pl.ds(1, 2)]
        if which == 1:
            return pltpu.make_async_copy(source, target, pair_send.at[h, 1])
        return remote(source, target, pair_send.at[h, 0], pair_recv.at[h], partner)

    def dq_copy(h, which):
        source, target = grad_out.at[h, which, 0], grads_ref.at[h, 0]
        if which == 1:
            return pltpu.make_async_copy(source, target, dq_send.at[h, 1])
        return remote(source, target, dq_send.at[h, 0], dq_recv.at[h], partner)

    @pl.when(is_inner)
    def _():
        ends_copy(me, 1, opp).start()

        def own_to_opp(h):
            own_copy(h, 0).wait()
            own_copy(h, 1).wait()
            qg_copy(h, me, 1, opp).start()

        @pl.loop(0, AHEAD)
        def _(h):
            own_to_opp(h)

        ends_copy(partner, 0, partner).wait_recv()
        ends_copy(partner, 2, opp).start()

        def relay(h):
            qg_copy(h, partner, 0, partner).wait_recv()
            qg_copy(h, partner, 2, opp).start()

        relay(0)

        @pl.loop(AHEAD, heads)
        def _(h):
            own_to_opp(h)

        ends_copy(opp, 1, opp).wait_recv()
        ends_copy(cross, 2, opp).wait_recv()

        across = lax.broadcasted_iota(jnp.int32, (8, rows), 1)
        down = lax.broadcasted_iota(jnp.int32, (rows, 128), 0)
        for s in range(n):
            window_row = jnp.zeros((8, rows), jnp.int32)
            window_col = jnp.zeros((rows, 128), jnp.int32)
            for w in range(n):
                stop = ends[s, 0:1, w : w + 1]
                window_row = window_row + jnp.where(across >= stop, 1, 0)
                window_col = window_col + jnp.where(down >= stop, 1, 0)
            key_row[s] = (window_row * n + s) * rows + across
            key_col[s] = (window_col * n + s) * rows + down

        def finish(h, which):
            part_copy(h, which).wait_recv()
            far = part_in[h, which].astype(jnp.int32).astype(jnp.float32) * scale_in[h, which]
            grad_out[h, which, 0] = (near[h, which] + far).astype(jnp.bfloat16)
            dq_copy(h, which).start()

        def finish_outer(h):
            scale_copy(h).wait_recv()
            finish(h, 0)

        @pl.loop(0, heads)
        def _(h):
            for later in (2 * h + 1, 2 * h + 2):

                @pl.when(later < heads)
                def _():
                    relay(later)

            own_copy(h, 2).wait()
            own_copy(h, 3).wait()
            kv_copy(h, partner).wait_recv()
            key_all = kv[h, 0]
            value_all = kv[h, 1]
            def part(shard):
                grad = qg[h, 0, block(shard), :]
                weights = masked(scores(grad, value_all), shard, (2 * side, 2 * side + 1), True)
                return weighted(weights, key_all)

            for which, shard in enumerate((cross, opp)):
                qg_copy(h, shard, 2 - which, opp).wait_recv()
            for which, shard in enumerate((cross, opp)):
                far = part(shard)
                top = jnp.maximum(jnp.max(jnp.abs(far), axis=0, keepdims=True), 1e-30)
                part_out[h, which] = jnp.round(far * (32767.0 / top)).astype(jnp.int32).astype(jnp.int16)
                scale_out[h, which] = top * (1.0 / 32767.0)
                if which == 0:
                    part_copy(h, 0).start()
            scale_copy(h).start()

            @pl.when(h == heads - 1)
            def _():
                @pl.loop(0, heads)
                def _(held):
                    part_copy(held, 1).start()

            for which, shard in enumerate((partner, me)):
                near[h, which] = part(shard)
            grad_all = qg[h, 0]
            query_all = qg[h, 1]
            for which, shard in enumerate((partner, me)):
                key = kv[h, 0, half(shard), :]
                value = kv[h, 1, half(shard), :]
                shards = tuple(range(n))
                grad_out[h, which, 1] = weighted(
                    masked(scores(value, grad_all), shard, shards, False), query_all
                ).astype(jnp.bfloat16)
                grad_out[h, which, 2] = weighted(
                    masked(scores(key, query_all), shard, shards, False), grad_all
                ).astype(jnp.bfloat16)
                pair_copy(h, which).start()

            @pl.when(h >= LAG)
            def _():
                finish_outer(h - LAG)

        @pl.loop(heads - LAG, heads)
        def _(h):
            finish_outer(h)

        @pl.loop(0, heads)
        def _(h):
            finish(h, 1)

        ends_copy(me, 1, opp).wait_send()
        ends_copy(partner, 2, opp).wait_send()

        @pl.loop(0, heads)
        def _(h):
            qg_copy(h, me, 1, opp).wait_send()
            qg_copy(h, partner, 2, opp).wait_send()
            pair_copy(h, 0).wait_send()
            pair_copy(h, 1).wait()
            part_copy(h, 0).wait_send()
            part_copy(h, 1).wait_send()
            scale_copy(h).wait_send()
            dq_copy(h, 0).wait_send()
            dq_copy(h, 1).wait()

    @pl.when(is_outer)
    def _():
        ends_copy(me, 0, partner).wait_send()

        @pl.loop(0, heads)
        def _(h):
            qg_copy(h, me, 0, partner).wait_send()
            kv_copy(h, me).wait_send()
            pair_copy(h, 0).wait_recv()
            dq_copy(h, 0).wait_recv()


def place_kernel(heads, grads_ref, dq_ref, dk_ref, dv_ref, sem):
    copies = [
        pltpu.make_async_copy(
            grads_ref.at[h, i], target.at[0, :, pl.ds(h * DH, DH)], sem.at[h, i]
        )
        for h in range(heads)
        for i, target in enumerate((dq_ref, dk_ref, dv_ref))
    ]
    for copy in copies:
        copy.start()
    for copy in copies:
        copy.wait()


def by_line(queries, keys, values, grad_output, counts):
    n = 4
    rows, width = queries.shape[1:]
    heads = width // DH
    dma = pltpu.SemaphoreType.DMA
    anywhere = pl.BlockSpec(memory_space=pl.ANY)
    packed = pl.pallas_call(
        functools.partial(line_kernel, rows, heads),
        out_shape=jax.ShapeDtypeStruct((heads, 3, rows, DH), jnp.bfloat16),
        in_specs=[pl.BlockSpec(memory_space=pltpu.HBM)] * 5,
        out_specs=anywhere,
        scratch_shapes=[
            pltpu.VMEM((heads, 2, n * rows, DH), jnp.bfloat16),
            pltpu.VMEM((heads, 2, 2 * rows, DH), jnp.bfloat16),
            pltpu.VMEM((1, 1, n), jnp.int32),
            pltpu.VMEM((n, 8, 128), jnp.int32),
            pltpu.VMEM((n, 8, rows), jnp.int32),
            pltpu.VMEM((n, rows, 128), jnp.int32),
            pltpu.VMEM((heads, 2, rows, DH), jnp.float32),
            pltpu.VMEM((heads, 2, 3, rows, DH), jnp.bfloat16),
            pltpu.VMEM((heads, 2, rows, DH), jnp.int16),
            pltpu.VMEM((heads, 2, rows, DH), jnp.int16),
            pltpu.VMEM((heads, 2, 1, DH), jnp.float32),
            pltpu.VMEM((heads, 2, 1, DH), jnp.float32),
            dma(()),
            dma((heads, 4)),
            dma((3,)),
            dma((3,)),
            dma((heads, 3)),
            dma((heads, 3)),
            dma((heads,)),
            dma((heads,)),
            dma((heads, 2)),
            dma((heads,)),
            dma((heads, 2)),
            dma((heads,)),
            dma((heads, 2)),
            dma((heads, 2)),
            dma((heads,)),
            dma((heads,)),
        ],
        compiler_params=pltpu.CompilerParams(collective_id=0, has_side_effects=True, vmem_limit_bytes=VMEM_LIMIT),
    )(*(pltpu.with_memory_space_constraint(x, pltpu.HBM) for x in (queries, keys, values, grad_output, counts)))
    return pl.pallas_call(
        functools.partial(place_kernel, heads),
        out_shape=[jax.ShapeDtypeStruct(queries.shape, jnp.bfloat16)] * 3,
        in_specs=[anywhere],
        out_specs=[anywhere] * 3,
        scratch_shapes=[dma((heads, 3))],
        compiler_params=pltpu.CompilerParams(vmem_limit_bytes=VMEM_LIMIT),
    )(packed)


def per_shard(queries, keys, values, grad_output, counts):
    n = lax.axis_size("seq")
    if n == 4 and queries.shape[1] == 128:
        return by_line(queries, keys, values, grad_output, counts)
    return per_device(queries, keys, values, grad_output, counts)


def solution(mesh):
    placed = (
        P(("groups", "dp"), "seq", "mp"),
        P(("groups", "dp"), "seq", "mp"),
        P(("groups", "dp"), "seq", "mp"),
        P(("groups", "dp"), "seq", "mp"),
        P(("groups", "dp"), "seq", None),
    )
    return jax.shard_map(
        per_shard,
        mesh=mesh,
        in_specs=placed,
        out_specs=(
            P(("groups", "dp"), "seq", "mp"),
            P(("groups", "dp"), "seq", "mp"),
            P(("groups", "dp"), "seq", "mp"),
        ),
        check_vma=False,
    )
```

```python
import functools
import math

import jax
import jax.numpy as jnp
from jax import lax
from jax.experimental import pallas as pl
from jax.experimental.pallas import tpu as pltpu
from jax.sharding import PartitionSpec as P

DH = 128


highest = lax.Precision.HIGHEST


def entering(value, axis, join, neutral, backward):
    count, mine = (lax.axis_size(axis), lax.axis_index(axis))
    pieces = lax.all_gather(value, axis)
    if backward:
        pieces = pieces[::-1]
        mine = count - 1 - mine
    total = jnp.full_like(value, 0) + jnp.asarray(neutral, value.dtype)

    def hop(position, total):
        longer = join(total, pieces[position])
        return jnp.where(position < mine, longer, total)

    return lax.fori_loop(0, count - 1, hop, total)


def add_states(earlier, later):
    return earlier + later


def per_device(queries, keys, values, grad_output, counts):
    shard_count = lax.axis_size("seq")
    local_rows = queries.shape[1]
    width = queries.shape[2]
    local_heads = width // DH
    capacity = 2 * local_rows // shard_count
    window_rows = shard_count * capacity
    factor = 1.0 / math.sqrt(DH * local_rows * shard_count)
    my_counts = counts[0, 0]
    upto = jnp.arange(shard_count)[:, None] >= jnp.arange(shard_count)[None, :]
    window_ends = jnp.sum(jnp.where(upto, my_counts[None, :], 0), axis=1)
    window_starts = window_ends - my_counts
    offsets = jnp.arange(capacity, dtype=jnp.int32)
    occupied = offsets[None, :] < my_counts[:, None]
    picked = jnp.where(occupied, window_starts[:, None] + offsets[None, :], 0).reshape(-1)
    occupied_column = occupied.reshape(-1, 1)

    def pack(source):
        taken = jnp.take(source[0], picked, axis=0)
        taken = jnp.where(occupied_column, taken, jnp.zeros_like(taken))
        return taken.reshape(shard_count, capacity, width)

    def split_heads(received):
        return received.reshape(window_rows, local_heads, DH)

    def outer_sum(left, right):
        return jnp.einsum("lha,lhb->hab", left, right, preferred_element_type=jnp.float32)

    query_recv, key_recv, value_recv, grad_recv = (
        lax.all_to_all(pack(queries), "seq", split_axis=0, concat_axis=0, tiled=True),
        lax.all_to_all(pack(keys), "seq", split_axis=0, concat_axis=0, tiled=True),
        lax.all_to_all(pack(values), "seq", split_axis=0, concat_axis=0, tiled=True),
        lax.all_to_all(pack(grad_output), "seq", split_axis=0, concat_axis=0, tiled=True),
    )
    query_recv = split_heads(query_recv)
    key_recv = split_heads(key_recv)
    value_recv = split_heads(value_recv)
    grad_recv = split_heads(grad_recv)
    key_state = outer_sum(key_recv, value_recv)
    query_state = outer_sum(query_recv, grad_recv)
    zero_state = jnp.zeros((local_heads, DH, DH), jnp.float32)
    before_kv = entering(key_state, "seq", add_states, zero_state, False)
    after_qd = entering(query_state, "seq", add_states, zero_state, True)
    block = min(512, window_rows)
    nblocks = window_rows // block

    def blocked(received):
        return received.reshape(nblocks, block, local_heads, DH)

    query_blocks = blocked(query_recv)
    key_blocks = blocked(key_recv)
    value_blocks = blocked(value_recv)
    grad_blocks = blocked(grad_recv)
    block_kv = jnp.einsum(
        "nlha,nlhb->nhab", key_blocks, value_blocks, preferred_element_type=jnp.float32
    )
    block_qd = jnp.einsum(
        "nlha,nlhb->nhab", query_blocks, grad_blocks, preferred_element_type=jnp.float32
    )
    kv_before = before_kv[None] + jnp.cumsum(block_kv, axis=0) - block_kv
    qd_after = after_qd[None] + jnp.sum(block_qd, axis=0)[None] - jnp.cumsum(block_qd, axis=0)
    lower = (
        lax.broadcasted_iota(jnp.int32, (block, block), 0)
        >= lax.broadcasted_iota(jnp.int32, (block, block), 1)
    ).astype(jnp.float32)

    def one_block(pieces):
        query_part, key_part, value_part, grad_part, kv_state, qd_state = pieces
        weights = (
            jnp.einsum("rha,sha->hrs", grad_part, value_part, preferred_element_type=jnp.float32)
            * lower[None]
        )
        scores = (
            jnp.einsum("rha,sha->hrs", query_part, key_part, preferred_element_type=jnp.float32)
            * lower[None]
        )
        query_f = query_part.astype(jnp.float32)
        key_f = key_part.astype(jnp.float32)
        value_f = value_part.astype(jnp.float32)
        grad_f = grad_part.astype(jnp.float32)
        grad_q = jnp.einsum("rhb,hab->rha", grad_f, kv_state, precision=highest) + jnp.einsum(
            "hrs,sha->rha", weights, key_f, precision=highest
        )
        grad_k = jnp.einsum("shb,hab->sha", value_f, qd_state, precision=highest) + jnp.einsum(
            "hrs,rha->sha", weights, query_f, precision=highest
        )
        grad_v = jnp.einsum("sha,hab->shb", key_f, qd_state, precision=highest) + jnp.einsum(
            "hrs,rhb->shb", scores, grad_f, precision=highest
        )

        def finish(result):
            return (result * factor).astype(jnp.bfloat16).reshape(block, width)

        return (finish(grad_q), finish(grad_k), finish(grad_v))

    out_q, out_k, out_v = lax.map(
        one_block, (query_blocks, key_blocks, value_blocks, grad_blocks, kv_before, qd_after)
    )

    def to_slots(result):
        return result.reshape(shard_count, capacity, width)

    back_q, back_k, back_v = (
        lax.all_to_all(to_slots(out_q), "seq", split_axis=0, concat_axis=0, tiled=True),
        lax.all_to_all(to_slots(out_k), "seq", split_axis=0, concat_axis=0, tiled=True),
        lax.all_to_all(to_slots(out_v), "seq", split_axis=0, concat_axis=0, tiled=True),
    )
    positions = jnp.arange(local_rows, dtype=jnp.int32)
    member = (
        (positions[:, None] >= window_starts[None, :]) & (positions[:, None] < window_ends[None, :])
    ).astype(jnp.int32)
    window_of = jnp.sum(member * jnp.arange(shard_count, dtype=jnp.int32)[None, :], axis=1)
    start_of = jnp.sum(member * window_starts[None, :], axis=1)
    source_index = window_of * capacity + positions - start_of

    def unpack(returned):
        return jnp.take(returned.reshape(window_rows, width), source_index, axis=0)[None]

    return (unpack(back_q), unpack(back_k), unpack(back_v))


MESH = pl.DeviceIdType.MESH
VMEM_LIMIT = 16 << 20


AHEAD = 4
LAG = 2


def line_kernel(
    rows,
    heads,
    q_ref,
    k_ref,
    v_ref,
    g_ref,
    counts_ref,
    grads_ref,
    qg,
    kv,
    mine,
    ends,
    key_row,
    key_col,
    near,
    grad_out,
    part_out,
    part_in,
    scale_out,
    scale_in,
    mine_sem,
    own_sem,
    ends_send,
    ends_recv,
    qg_send,
    qg_recv,
    kv_send,
    kv_recv,
    pair_send,
    pair_recv,
    dq_send,
    dq_recv,
    part_send,
    part_recv,
    scale_send,
    scale_recv,
):
    n = 4
    me = lax.axis_index("seq")
    factor = 1.0 / math.sqrt(DH * n * rows)
    side = me // 2
    partner = me + 1 - 2 * lax.rem(me, 2)
    opp = n - 1 - me
    cross = n - 1 - partner
    is_inner = jnp.logical_or(me == 1, me == 2)
    is_outer = jnp.logical_not(is_inner)

    def columns(head):
        return pl.ds(pl.multiple_of(head * DH, DH), DH)

    def block(shard):
        return pl.ds(pl.multiple_of(shard * rows, rows), rows)

    def half(shard):
        return block(lax.rem(shard, 2))

    def remote(source, target, send, recv, device):
        return pltpu.make_async_remote_copy(
            src_ref=source,
            dst_ref=target,
            send_sem=send,
            recv_sem=recv,
            device_id={"seq": device},
            device_id_type=MESH,
        )

    barrier = pltpu.get_barrier_semaphore()
    pl.semaphore_signal(barrier, inc=1, device_id={"seq": partner}, device_id_type=MESH)

    @pl.when(is_inner)
    def _():
        pl.semaphore_signal(barrier, inc=1, device_id={"seq": opp}, device_id_type=MESH)

    load = pltpu.make_async_copy(counts_ref, mine, mine_sem)
    load.start()

    def own_copy(h, i):
        source = (g_ref, q_ref, k_ref, v_ref)[i].at[0, :, columns(h)]
        target = qg.at[h, i, block(me)] if i < 2 else kv.at[h, i - 2, half(me)]
        return pltpu.make_async_copy(source, target, own_sem.at[h, i])

    @pl.loop(0, heads)
    def _(h):
        for i in range(4):
            own_copy(h, i).start()

    load.wait()
    lanes = lax.broadcasted_iota(jnp.int32, (8, 128), 1)
    end = jnp.zeros((1, 1), jnp.int32)
    table = jnp.zeros((8, 128), jnp.int32)
    for w in range(n):
        end = end + mine[0, 0:1, w : w + 1]
        table = jnp.where(lanes == w, end, table)
    ends[me] = table

    pl.semaphore_wait(barrier, jnp.where(is_inner, 2, 1))

    def ends_copy(shard, which, device):
        return remote(ends.at[shard], ends.at[shard], ends_send.at[which], ends_recv.at[which], device)

    def qg_copy(h, shard, which, device):
        at = qg.at[h, :, block(shard)]
        return remote(at, at, qg_send.at[h, which], qg_recv.at[h, which], device)

    def kv_copy(h, shard):
        at = kv.at[h, :, half(shard)]
        return remote(at, at, kv_send.at[h], kv_recv.at[h], partner)

    @pl.when(is_outer)
    def _():
        ends_copy(me, 0, partner).start()

        def give_qg(h):
            own_copy(h, 0).wait()
            own_copy(h, 1).wait()
            qg_copy(h, me, 0, partner).start()

        def give_kv(h):
            own_copy(h, 2).wait()
            own_copy(h, 3).wait()
            kv_copy(h, me).start()

        give_qg(0)

        @pl.loop(0, heads)
        def _(h):
            give_kv(h)
            for later in (2 * h + 1, 2 * h + 2):

                @pl.when(later < heads)
                def _():
                    give_qg(later)

    def scores(left, right):
        return lax.dot_general(
            left, right, (((1,), (1,)), ((), ())), preferred_element_type=jnp.float32
        )

    def weighted(weights, right):
        high = weights.astype(jnp.bfloat16)
        low = (weights - high.astype(jnp.float32)).astype(jnp.bfloat16)
        product = jnp.dot(high, right, preferred_element_type=jnp.float32) + jnp.dot(
            low, right, preferred_element_type=jnp.float32
        )
        return product * factor

    def masked(weights, at, others, forward):
        col = key_col[pl.ds(2 * at, 2)].reshape(2 * rows, 128)
        pieces = []
        for i, other in enumerate(others):
            row = key_row[other][0:1, :]
            keep = (row <= col) if forward else (row >= col)
            pieces.append(jnp.where(keep, weights[:, i * rows : (i + 1) * rows], 0.0))
        return jnp.concatenate(pieces, axis=1)

    def part_copy(h, which):
        return remote(
            part_out.at[h, which],
            part_in.at[h, which],
            part_send.at[h, which],
            part_recv.at[h, which],
            opp,
        )

    def scale_copy(h):
        return remote(scale_out.at[h], scale_in.at[h], scale_send.at[h], scale_recv.at[h], opp)

    def pair_copy(h, which):
        source, target = grad_out.at[h, which, pl.ds(1, 2)], grads_ref.at[h, pl.ds(1, 2)]
        if which == 1:
            return pltpu.make_async_copy(source, target, pair_send.at[h, 1])
        return remote(source, target, pair_send.at[h, 0], pair_recv.at[h], partner)

    def dq_copy(h, which):
        source, target = grad_out.at[h, which, 0], grads_ref.at[h, 0]
        if which == 1:
            return pltpu.make_async_copy(source, target, dq_send.at[h, 1])
        return remote(source, target, dq_send.at[h, 0], dq_recv.at[h], partner)

    @pl.when(is_inner)
    def _():
        ends_copy(me, 1, opp).start()

        def own_to_opp(h):
            own_copy(h, 0).wait()
            own_copy(h, 1).wait()
            qg_copy(h, me, 1, opp).start()

        @pl.loop(0, AHEAD)
        def _(h):
            own_to_opp(h)

        ends_copy(partner, 0, partner).wait_recv()
        ends_copy(partner, 2, opp).start()

        def relay(h):
            qg_copy(h, partner, 0, partner).wait_recv()
            qg_copy(h, partner, 2, opp).start()

        relay(0)

        @pl.loop(AHEAD, heads)
        def _(h):
            own_to_opp(h)

        ends_copy(opp, 1, opp).wait_recv()
        ends_copy(cross, 2, opp).wait_recv()

        across = lax.broadcasted_iota(jnp.int32, (8, rows), 1)
        down = lax.broadcasted_iota(jnp.int32, (rows, 128), 0)
        for s in range(n):
            window_row = jnp.zeros((8, rows), jnp.int32)
            window_col = jnp.zeros((rows, 128), jnp.int32)
            for w in range(n):
                stop = ends[s, 0:1, w : w + 1]
                window_row = window_row + jnp.where(across >= stop, 1, 0)
                window_col = window_col + jnp.where(down >= stop, 1, 0)
            key_row[s] = (window_row * n + s) * rows + across
            key_col[s] = (window_col * n + s) * rows + down

        def finish(h, which):
            part_copy(h, which).wait_recv()
            far = part_in[h, which].astype(jnp.int32).astype(jnp.float32) * scale_in[h, which]
            grad_out[h, which, 0] = (near[h, which] + far).astype(jnp.bfloat16)
            dq_copy(h, which).start()

        def finish_outer(h):
            scale_copy(h).wait_recv()
            finish(h, 0)

        @pl.loop(0, heads)
        def _(h):
            for later in (2 * h + 1, 2 * h + 2):

                @pl.when(later < heads)
                def _():
                    relay(later)

            own_copy(h, 2).wait()
            own_copy(h, 3).wait()
            kv_copy(h, partner).wait_recv()
            key_all = kv[h, 0]
            value_all = kv[h, 1]
            def part(at):
                grad = qg[h, 0, pl.ds(pl.multiple_of(2 * at * rows, 2 * rows), 2 * rows), :]
                weights = masked(scores(grad, value_all), at, (2 * side, 2 * side + 1), True)
                return weighted(weights, key_all)

            for which, shard in enumerate((cross, opp)):
                qg_copy(h, shard, 2 - which, opp).wait_recv()
            both = part(1 - side)
            for i in range(2):
                which = (1 - side) if i == 0 else side
                far = both[i * rows : (i + 1) * rows]
                top = jnp.maximum(jnp.max(jnp.abs(far), axis=0, keepdims=True), 1e-30)
                part_out[h, which] = jnp.round(far * (32767.0 / top)).astype(jnp.int32).astype(jnp.int16)
                scale_out[h, which] = top * (1.0 / 32767.0)
            part_copy(h, 0).start()
            scale_copy(h).start()

            @pl.when(h >= 4)
            def _():
                part_copy(h - 4, 1).start()

            both = part(side)
            for i in range(2):
                near[h, side if i == 0 else 1 - side] = both[i * rows : (i + 1) * rows]
            grad_all = qg[h, 0]
            query_all = qg[h, 1]
            shards = tuple(range(n))
            for j, left, over, right in (
                (1, value_all, grad_all, query_all),
                (2, key_all, query_all, grad_all),
            ):
                both = weighted(masked(scores(left, over), side, shards, False), right)
                for i in range(2):
                    which = side if i == 0 else 1 - side
                    grad_out[h, which, j] = both[i * rows : (i + 1) * rows].astype(jnp.bfloat16)
            for which in range(2):
                pair_copy(h, which).start()

            @pl.when(h == heads - 1)
            def _():
                @pl.loop(heads - 4, heads)
                def _(held):
                    part_copy(held, 1).start()

            @pl.when(h >= LAG)
            def _():
                finish_outer(h - LAG)

        @pl.loop(heads - LAG, heads)
        def _(h):
            finish_outer(h)

        @pl.loop(0, heads)
        def _(h):
            finish(h, 1)

        ends_copy(me, 1, opp).wait_send()
        ends_copy(partner, 2, opp).wait_send()

        @pl.loop(0, heads)
        def _(h):
            qg_copy(h, me, 1, opp).wait_send()
            qg_copy(h, partner, 2, opp).wait_send()
            pair_copy(h, 0).wait_send()
            pair_copy(h, 1).wait()
            part_copy(h, 0).wait_send()
            part_copy(h, 1).wait_send()
            scale_copy(h).wait_send()
            dq_copy(h, 0).wait_send()
            dq_copy(h, 1).wait()

    @pl.when(is_outer)
    def _():
        ends_copy(me, 0, partner).wait_send()

        @pl.loop(0, heads)
        def _(h):
            qg_copy(h, me, 0, partner).wait_send()
            kv_copy(h, me).wait_send()
            pair_copy(h, 0).wait_recv()
            dq_copy(h, 0).wait_recv()


def place_kernel(heads, grads_ref, dq_ref, dk_ref, dv_ref, sem):
    copies = [
        pltpu.make_async_copy(
            grads_ref.at[h, i], target.at[0, :, pl.ds(h * DH, DH)], sem.at[h, i]
        )
        for h in range(heads)
        for i, target in enumerate((dq_ref, dk_ref, dv_ref))
    ]
    for copy in copies:
        copy.start()
    for copy in copies:
        copy.wait()


def by_line(queries, keys, values, grad_output, counts):
    n = 4
    rows, width = queries.shape[1:]
    heads = width // DH
    dma = pltpu.SemaphoreType.DMA
    anywhere = pl.BlockSpec(memory_space=pl.ANY)
    packed = pl.pallas_call(
        functools.partial(line_kernel, rows, heads),
        out_shape=jax.ShapeDtypeStruct((heads, 3, rows, DH), jnp.bfloat16),
        in_specs=[pl.BlockSpec(memory_space=pltpu.HBM)] * 5,
        out_specs=anywhere,
        scratch_shapes=[
            pltpu.VMEM((heads, 2, n * rows, DH), jnp.bfloat16),
            pltpu.VMEM((heads, 2, 2 * rows, DH), jnp.bfloat16),
            pltpu.VMEM((1, 1, n), jnp.int32),
            pltpu.VMEM((n, 8, 128), jnp.int32),
            pltpu.VMEM((n, 8, rows), jnp.int32),
            pltpu.VMEM((n, rows, 128), jnp.int32),
            pltpu.VMEM((heads, 2, rows, DH), jnp.float32),
            pltpu.VMEM((heads, 2, 3, rows, DH), jnp.bfloat16),
            pltpu.VMEM((heads, 2, rows, DH), jnp.int16),
            pltpu.VMEM((heads, 2, rows, DH), jnp.int16),
            pltpu.VMEM((heads, 2, 1, DH), jnp.float32),
            pltpu.VMEM((heads, 2, 1, DH), jnp.float32),
            dma(()),
            dma((heads, 4)),
            dma((3,)),
            dma((3,)),
            dma((heads, 3)),
            dma((heads, 3)),
            dma((heads,)),
            dma((heads,)),
            dma((heads, 2)),
            dma((heads,)),
            dma((heads, 2)),
            dma((heads,)),
            dma((heads, 2)),
            dma((heads, 2)),
            dma((heads,)),
            dma((heads,)),
        ],
        compiler_params=pltpu.CompilerParams(collective_id=0, has_side_effects=True, vmem_limit_bytes=VMEM_LIMIT),
    )(*(pltpu.with_memory_space_constraint(x, pltpu.HBM) for x in (queries, keys, values, grad_output, counts)))
    return pl.pallas_call(
        functools.partial(place_kernel, heads),
        out_shape=[jax.ShapeDtypeStruct(queries.shape, jnp.bfloat16)] * 3,
        in_specs=[anywhere],
        out_specs=[anywhere] * 3,
        scratch_shapes=[dma((heads, 3))],
        compiler_params=pltpu.CompilerParams(vmem_limit_bytes=VMEM_LIMIT),
    )(packed)


def per_shard(queries, keys, values, grad_output, counts):
    n = lax.axis_size("seq")
    if n == 4 and queries.shape[1] == 128:
        return by_line(queries, keys, values, grad_output, counts)
    return per_device(queries, keys, values, grad_output, counts)


def solution(mesh):
    placed = (
        P(("groups", "dp"), "seq", "mp"),
        P(("groups", "dp"), "seq", "mp"),
        P(("groups", "dp"), "seq", "mp"),
        P(("groups", "dp"), "seq", "mp"),
        P(("groups", "dp"), "seq", None),
    )
    return jax.shard_map(
        per_shard,
        mesh=mesh,
        in_specs=placed,
        out_specs=(
            P(("groups", "dp"), "seq", "mp"),
            P(("groups", "dp"), "seq", "mp"),
            P(("groups", "dp"), "seq", "mp"),
        ),
        check_vma=False,
    )
```

```python
import functools
import math

import jax
import jax.numpy as jnp
from jax import lax
from jax.experimental import pallas as pl
from jax.experimental.pallas import tpu as pltpu
from jax.sharding import PartitionSpec as P

DH = 128


highest = lax.Precision.HIGHEST


def entering(value, axis, join, neutral, backward):
    count, mine = (lax.axis_size(axis), lax.axis_index(axis))
    pieces = lax.all_gather(value, axis)
    if backward:
        pieces = pieces[::-1]
        mine = count - 1 - mine
    total = jnp.full_like(value, 0) + jnp.asarray(neutral, value.dtype)

    def hop(position, total):
        longer = join(total, pieces[position])
        return jnp.where(position < mine, longer, total)

    return lax.fori_loop(0, count - 1, hop, total)


def add_states(earlier, later):
    return earlier + later


def per_device(queries, keys, values, grad_output, counts):
    shard_count = lax.axis_size("seq")
    local_rows = queries.shape[1]
    width = queries.shape[2]
    local_heads = width // DH
    capacity = 2 * local_rows // shard_count
    window_rows = shard_count * capacity
    factor = 1.0 / math.sqrt(DH * local_rows * shard_count)
    my_counts = counts[0, 0]
    upto = jnp.arange(shard_count)[:, None] >= jnp.arange(shard_count)[None, :]
    window_ends = jnp.sum(jnp.where(upto, my_counts[None, :], 0), axis=1)
    window_starts = window_ends - my_counts
    offsets = jnp.arange(capacity, dtype=jnp.int32)
    occupied = offsets[None, :] < my_counts[:, None]
    picked = jnp.where(occupied, window_starts[:, None] + offsets[None, :], 0).reshape(-1)
    occupied_column = occupied.reshape(-1, 1)

    def pack(source):
        taken = jnp.take(source[0], picked, axis=0)
        taken = jnp.where(occupied_column, taken, jnp.zeros_like(taken))
        return taken.reshape(shard_count, capacity, width)

    def split_heads(received):
        return received.reshape(window_rows, local_heads, DH)

    def outer_sum(left, right):
        return jnp.einsum("lha,lhb->hab", left, right, preferred_element_type=jnp.float32)

    query_recv, key_recv, value_recv, grad_recv = (
        lax.all_to_all(pack(queries), "seq", split_axis=0, concat_axis=0, tiled=True),
        lax.all_to_all(pack(keys), "seq", split_axis=0, concat_axis=0, tiled=True),
        lax.all_to_all(pack(values), "seq", split_axis=0, concat_axis=0, tiled=True),
        lax.all_to_all(pack(grad_output), "seq", split_axis=0, concat_axis=0, tiled=True),
    )
    query_recv = split_heads(query_recv)
    key_recv = split_heads(key_recv)
    value_recv = split_heads(value_recv)
    grad_recv = split_heads(grad_recv)
    key_state = outer_sum(key_recv, value_recv)
    query_state = outer_sum(query_recv, grad_recv)
    zero_state = jnp.zeros((local_heads, DH, DH), jnp.float32)
    before_kv = entering(key_state, "seq", add_states, zero_state, False)
    after_qd = entering(query_state, "seq", add_states, zero_state, True)
    block = min(512, window_rows)
    nblocks = window_rows // block

    def blocked(received):
        return received.reshape(nblocks, block, local_heads, DH)

    query_blocks = blocked(query_recv)
    key_blocks = blocked(key_recv)
    value_blocks = blocked(value_recv)
    grad_blocks = blocked(grad_recv)
    block_kv = jnp.einsum(
        "nlha,nlhb->nhab", key_blocks, value_blocks, preferred_element_type=jnp.float32
    )
    block_qd = jnp.einsum(
        "nlha,nlhb->nhab", query_blocks, grad_blocks, preferred_element_type=jnp.float32
    )
    kv_before = before_kv[None] + jnp.cumsum(block_kv, axis=0) - block_kv
    qd_after = after_qd[None] + jnp.sum(block_qd, axis=0)[None] - jnp.cumsum(block_qd, axis=0)
    lower = (
        lax.broadcasted_iota(jnp.int32, (block, block), 0)
        >= lax.broadcasted_iota(jnp.int32, (block, block), 1)
    ).astype(jnp.float32)

    def one_block(pieces):
        query_part, key_part, value_part, grad_part, kv_state, qd_state = pieces
        weights = (
            jnp.einsum("rha,sha->hrs", grad_part, value_part, preferred_element_type=jnp.float32)
            * lower[None]
        )
        scores = (
            jnp.einsum("rha,sha->hrs", query_part, key_part, preferred_element_type=jnp.float32)
            * lower[None]
        )
        query_f = query_part.astype(jnp.float32)
        key_f = key_part.astype(jnp.float32)
        value_f = value_part.astype(jnp.float32)
        grad_f = grad_part.astype(jnp.float32)
        grad_q = jnp.einsum("rhb,hab->rha", grad_f, kv_state, precision=highest) + jnp.einsum(
            "hrs,sha->rha", weights, key_f, precision=highest
        )
        grad_k = jnp.einsum("shb,hab->sha", value_f, qd_state, precision=highest) + jnp.einsum(
            "hrs,rha->sha", weights, query_f, precision=highest
        )
        grad_v = jnp.einsum("sha,hab->shb", key_f, qd_state, precision=highest) + jnp.einsum(
            "hrs,rhb->shb", scores, grad_f, precision=highest
        )

        def finish(result):
            return (result * factor).astype(jnp.bfloat16).reshape(block, width)

        return (finish(grad_q), finish(grad_k), finish(grad_v))

    out_q, out_k, out_v = lax.map(
        one_block, (query_blocks, key_blocks, value_blocks, grad_blocks, kv_before, qd_after)
    )

    def to_slots(result):
        return result.reshape(shard_count, capacity, width)

    back_q, back_k, back_v = (
        lax.all_to_all(to_slots(out_q), "seq", split_axis=0, concat_axis=0, tiled=True),
        lax.all_to_all(to_slots(out_k), "seq", split_axis=0, concat_axis=0, tiled=True),
        lax.all_to_all(to_slots(out_v), "seq", split_axis=0, concat_axis=0, tiled=True),
    )
    positions = jnp.arange(local_rows, dtype=jnp.int32)
    member = (
        (positions[:, None] >= window_starts[None, :]) & (positions[:, None] < window_ends[None, :])
    ).astype(jnp.int32)
    window_of = jnp.sum(member * jnp.arange(shard_count, dtype=jnp.int32)[None, :], axis=1)
    start_of = jnp.sum(member * window_starts[None, :], axis=1)
    source_index = window_of * capacity + positions - start_of

    def unpack(returned):
        return jnp.take(returned.reshape(window_rows, width), source_index, axis=0)[None]

    return (unpack(back_q), unpack(back_k), unpack(back_v))


MESH = pl.DeviceIdType.MESH
VMEM_LIMIT = 16 << 20


AHEAD = 4
LAG = 3


def line_kernel(
    rows,
    heads,
    q_ref,
    k_ref,
    v_ref,
    g_ref,
    counts_ref,
    grads_ref,
    qg,
    kv,
    mine,
    ends,
    key_row,
    key_col,
    near,
    grad_out,
    part_out,
    part_in,
    scale_out,
    scale_in,
    mine_sem,
    own_sem,
    ends_send,
    ends_recv,
    qg_send,
    qg_recv,
    kv_send,
    kv_recv,
    pair_send,
    pair_recv,
    dq_send,
    dq_recv,
    part_send,
    part_recv,
    scale_send,
    scale_recv,
):
    n = 4
    me = lax.axis_index("seq")
    factor = 1.0 / math.sqrt(DH * n * rows)
    side = me // 2
    partner = me + 1 - 2 * lax.rem(me, 2)
    opp = n - 1 - me
    cross = n - 1 - partner
    is_inner = jnp.logical_or(me == 1, me == 2)
    is_outer = jnp.logical_not(is_inner)

    def columns(head):
        return pl.ds(pl.multiple_of(head * DH, DH), DH)

    def block(shard):
        return pl.ds(pl.multiple_of(shard * rows, rows), rows)

    def half(shard):
        return block(lax.rem(shard, 2))

    def remote(source, target, send, recv, device):
        return pltpu.make_async_remote_copy(
            src_ref=source,
            dst_ref=target,
            send_sem=send,
            recv_sem=recv,
            device_id={"seq": device},
            device_id_type=MESH,
        )

    barrier = pltpu.get_barrier_semaphore()
    pl.semaphore_signal(barrier, inc=1, device_id={"seq": partner}, device_id_type=MESH)

    @pl.when(is_inner)
    def _():
        pl.semaphore_signal(barrier, inc=1, device_id={"seq": opp}, device_id_type=MESH)

    load = pltpu.make_async_copy(counts_ref, mine, mine_sem)
    load.start()

    def own_copy(h, i):
        source = (g_ref, q_ref, k_ref, v_ref)[i].at[0, :, columns(h)]
        target = qg.at[h, i, block(me)] if i < 2 else kv.at[h, i - 2, half(me)]
        return pltpu.make_async_copy(source, target, own_sem.at[h, i])

    @pl.loop(0, heads)
    def _(h):
        for i in range(4):
            own_copy(h, i).start()

    load.wait()
    lanes = lax.broadcasted_iota(jnp.int32, (8, 128), 1)
    end = jnp.zeros((1, 1), jnp.int32)
    table = jnp.zeros((8, 128), jnp.int32)
    for w in range(n):
        end = end + mine[0, 0:1, w : w + 1]
        table = jnp.where(lanes == w, end, table)
    ends[me] = table

    pl.semaphore_wait(barrier, jnp.where(is_inner, 2, 1))

    def ends_copy(shard, which, device):
        return remote(ends.at[shard], ends.at[shard], ends_send.at[which], ends_recv.at[which], device)

    def qg_copy(h, shard, which, device):
        at = qg.at[h, :, block(shard)]
        return remote(at, at, qg_send.at[h, which], qg_recv.at[h, which], device)

    def group_copy(h, shard):
        at = qg.at[pl.ds(h, 4), :, block(shard)]
        return remote(at, at, qg_send.at[h, 1], qg_recv.at[h, 1], opp)

    def kv_copy(h, shard):
        at = kv.at[h, :, half(shard)]
        return remote(at, at, kv_send.at[h], kv_recv.at[h], partner)

    @pl.when(is_outer)
    def _():
        ends_copy(me, 0, partner).start()

        def give_qg(h):
            own_copy(h, 0).wait()
            own_copy(h, 1).wait()
            qg_copy(h, me, 0, partner).start()

        def give_kv(h):
            own_copy(h, 2).wait()
            own_copy(h, 3).wait()
            kv_copy(h, me).start()

        give_qg(0)

        @pl.loop(0, heads)
        def _(h):
            give_kv(h)
            for later in (2 * h + 1, 2 * h + 2):

                @pl.when(later < heads)
                def _():
                    give_qg(later)

    def scores(left, right):
        return lax.dot_general(
            left, right, (((1,), (1,)), ((), ())), preferred_element_type=jnp.float32
        )

    def weighted(weights, right):
        high = weights.astype(jnp.bfloat16)
        low = (weights - high.astype(jnp.float32)).astype(jnp.bfloat16)
        product = jnp.dot(high, right, preferred_element_type=jnp.float32) + jnp.dot(
            low, right, preferred_element_type=jnp.float32
        )
        return product * factor

    def masked(weights, at, others, forward):
        col = key_col[pl.ds(2 * at, 2)].reshape(2 * rows, 128)
        pieces = []
        for i, other in enumerate(others):
            row = key_row[other][0:1, :]
            keep = (row <= col) if forward else (row >= col)
            pieces.append(jnp.where(keep, weights[:, i * rows : (i + 1) * rows], 0.0))
        return jnp.concatenate(pieces, axis=1)

    def part_copy(h, which):
        return remote(
            part_out.at[h, which],
            part_in.at[h, which],
            part_send.at[h, which],
            part_recv.at[h, which],
            opp,
        )

    def scale_copy(h):
        return remote(scale_out.at[h], scale_in.at[h], scale_send.at[h], scale_recv.at[h], opp)

    def pair_copy(h, which):
        source, target = grad_out.at[h, which, pl.ds(1, 2)], grads_ref.at[pl.ds(1, 2), :, columns(h)]
        if which == 1:
            return pltpu.make_async_copy(source, target, pair_send.at[h, 1])
        return remote(source, target, pair_send.at[h, 0], pair_recv.at[h], partner)

    def dq_copy(h, which):
        source, target = grad_out.at[h, which, 0], grads_ref.at[0, :, columns(h)]
        if which == 1:
            return pltpu.make_async_copy(source, target, dq_send.at[h, 1])
        return remote(source, target, dq_send.at[h, 0], dq_recv.at[h], partner)

    @pl.when(is_inner)
    def _():
        ends_copy(me, 1, opp).start()

        def group_to_opp(first):
            @pl.loop(first, first + 4)
            def _(h):
                own_copy(h, 0).wait()
                own_copy(h, 1).wait()

            group_copy(first, me).start()

        group_to_opp(0)

        ends_copy(partner, 0, partner).wait_recv()
        ends_copy(partner, 2, opp).start()

        def relay(h):
            qg_copy(h, partner, 0, partner).wait_recv()
            qg_copy(h, partner, 2, opp).start()

        relay(0)

        for first in range(4, heads, 4):
            group_to_opp(first)

        ends_copy(opp, 1, opp).wait_recv()
        ends_copy(cross, 2, opp).wait_recv()

        across = lax.broadcasted_iota(jnp.int32, (8, rows), 1)
        down = lax.broadcasted_iota(jnp.int32, (rows, 128), 0)
        for s in range(n):
            window_row = jnp.zeros((8, rows), jnp.int32)
            window_col = jnp.zeros((rows, 128), jnp.int32)
            for w in range(n):
                stop = ends[s, 0:1, w : w + 1]
                window_row = window_row + jnp.where(across >= stop, 1, 0)
                window_col = window_col + jnp.where(down >= stop, 1, 0)
            key_row[s] = (window_row * n + s) * rows + across
            key_col[s] = (window_col * n + s) * rows + down

        def finish(h, which):
            part_copy(h, which).wait_recv()
            far = part_in[h, which].astype(jnp.int32).astype(jnp.float32) * scale_in[h, which]
            grad_out[h, which, 0] = (near[h, which] + far).astype(jnp.bfloat16)
            dq_copy(h, which).start()

        def finish_outer(h):
            scale_copy(h).wait_recv()
            finish(h, 0)

        @pl.loop(0, heads)
        def _(h):
            for later in (2 * h + 1, 2 * h + 2):

                @pl.when(later < heads)
                def _():
                    relay(later)

            own_copy(h, 2).wait()
            own_copy(h, 3).wait()
            kv_copy(h, partner).wait_recv()
            key_all = kv[h, 0]
            value_all = kv[h, 1]
            def part(at):
                grad = qg[h, 0, pl.ds(pl.multiple_of(2 * at * rows, 2 * rows), 2 * rows), :]
                weights = masked(scores(grad, value_all), at, (2 * side, 2 * side + 1), True)
                return weighted(weights, key_all)

            @pl.when(lax.rem(h, 4) == 0)
            def _():
                group_copy(h, opp).wait_recv()

            qg_copy(h, cross, 2, opp).wait_recv()
            both = part(1 - side)
            for i in range(2):
                which = (1 - side) if i == 0 else side
                far = both[i * rows : (i + 1) * rows]
                top = jnp.maximum(jnp.max(jnp.abs(far), axis=0, keepdims=True), 1e-30)
                part_out[h, which] = jnp.round(far * (32767.0 / top)).astype(jnp.int32).astype(jnp.int16)
                scale_out[h, which] = top * (1.0 / 32767.0)
            part_copy(h, 0).start()
            scale_copy(h).start()

            @pl.when(h >= 4)
            def _():
                part_copy(h - 4, 1).start()

            both = part(side)
            for i in range(2):
                near[h, side if i == 0 else 1 - side] = both[i * rows : (i + 1) * rows]
            grad_all = qg[h, 0]
            query_all = qg[h, 1]
            shards = tuple(range(n))
            for j, left, over, right in (
                (1, value_all, grad_all, query_all),
                (2, key_all, query_all, grad_all),
            ):
                both = weighted(masked(scores(left, over), side, shards, False), right)
                for i in range(2):
                    which = side if i == 0 else 1 - side
                    grad_out[h, which, j] = both[i * rows : (i + 1) * rows].astype(jnp.bfloat16)
            for which in range(2):
                pair_copy(h, which).start()

            @pl.when(h == heads - 1)
            def _():
                @pl.loop(heads - 4, heads)
                def _(held):
                    part_copy(held, 1).start()

            @pl.when(h >= LAG)
            def _():
                finish_outer(h - LAG)

        @pl.loop(heads - LAG, heads)
        def _(h):
            finish_outer(h)

        @pl.loop(0, heads)
        def _(h):
            finish(h, 1)

        ends_copy(me, 1, opp).wait_send()
        ends_copy(partner, 2, opp).wait_send()

        @pl.loop(0, heads)
        def _(h):
            @pl.when(lax.rem(h, 4) == 0)
            def _():
                group_copy(h, me).wait_send()

            qg_copy(h, partner, 2, opp).wait_send()
            pair_copy(h, 0).wait_send()
            pair_copy(h, 1).wait()
            part_copy(h, 0).wait_send()
            part_copy(h, 1).wait_send()
            scale_copy(h).wait_send()
            dq_copy(h, 0).wait_send()
            dq_copy(h, 1).wait()

    @pl.when(is_outer)
    def _():
        ends_copy(me, 0, partner).wait_send()

        @pl.loop(0, heads)
        def _(h):
            qg_copy(h, me, 0, partner).wait_send()
            kv_copy(h, me).wait_send()
            pair_copy(h, 0).wait_recv()
            dq_copy(h, 0).wait_recv()


def place_kernel(grads_ref, dq_ref, dk_ref, dv_ref, sem):
    copies = [
        pltpu.make_async_copy(grads_ref.at[i], target.at[0], sem.at[i])
        for i, target in enumerate((dq_ref, dk_ref, dv_ref))
    ]
    for copy in copies:
        copy.start()
    for copy in copies:
        copy.wait()


def by_line(queries, keys, values, grad_output, counts):
    n = 4
    rows, width = queries.shape[1:]
    heads = width // DH
    dma = pltpu.SemaphoreType.DMA
    anywhere = pl.BlockSpec(memory_space=pl.ANY)
    packed = pl.pallas_call(
        functools.partial(line_kernel, rows, heads),
        out_shape=jax.ShapeDtypeStruct((3, rows, width), jnp.bfloat16),
        in_specs=[pl.BlockSpec(memory_space=pltpu.HBM)] * 5,
        out_specs=anywhere,
        scratch_shapes=[
            pltpu.VMEM((heads, 2, n * rows, DH), jnp.bfloat16),
            pltpu.VMEM((heads, 2, 2 * rows, DH), jnp.bfloat16),
            pltpu.VMEM((1, 1, n), jnp.int32),
            pltpu.VMEM((n, 8, 128), jnp.int32),
            pltpu.VMEM((n, 8, rows), jnp.int32),
            pltpu.VMEM((n, rows, 128), jnp.int32),
            pltpu.VMEM((heads, 2, rows, DH), jnp.float32),
            pltpu.VMEM((heads, 2, 3, rows, DH), jnp.bfloat16),
            pltpu.VMEM((heads, 2, rows, DH), jnp.int16),
            pltpu.VMEM((heads, 2, rows, DH), jnp.int16),
            pltpu.VMEM((heads, 2, 1, DH), jnp.float32),
            pltpu.VMEM((heads, 2, 1, DH), jnp.float32),
            dma(()),
            dma((heads, 4)),
            dma((3,)),
            dma((3,)),
            dma((heads, 3)),
            dma((heads, 3)),
            dma((heads,)),
            dma((heads,)),
            dma((heads, 2)),
            dma((heads,)),
            dma((heads, 2)),
            dma((heads,)),
            dma((heads, 2)),
            dma((heads, 2)),
            dma((heads,)),
            dma((heads,)),
        ],
        compiler_params=pltpu.CompilerParams(collective_id=0, has_side_effects=True, vmem_limit_bytes=VMEM_LIMIT),
    )(*(pltpu.with_memory_space_constraint(x, pltpu.HBM) for x in (queries, keys, values, grad_output, counts)))
    return pl.pallas_call(
        place_kernel,
        out_shape=[jax.ShapeDtypeStruct(queries.shape, jnp.bfloat16)] * 3,
        in_specs=[anywhere],
        out_specs=[anywhere] * 3,
        scratch_shapes=[dma((3,))],
        compiler_params=pltpu.CompilerParams(vmem_limit_bytes=VMEM_LIMIT),
    )(packed)


def per_shard(queries, keys, values, grad_output, counts):
    n = lax.axis_size("seq")
    if n == 4 and queries.shape[1] == 128:
        return by_line(queries, keys, values, grad_output, counts)
    return per_device(queries, keys, values, grad_output, counts)


def solution(mesh):
    placed = (
        P(("groups", "dp"), "seq", "mp"),
        P(("groups", "dp"), "seq", "mp"),
        P(("groups", "dp"), "seq", "mp"),
        P(("groups", "dp"), "seq", "mp"),
        P(("groups", "dp"), "seq", None),
    )
    return jax.shard_map(
        per_shard,
        mesh=mesh,
        in_specs=placed,
        out_specs=(
            P(("groups", "dp"), "seq", "mp"),
            P(("groups", "dp"), "seq", "mp"),
            P(("groups", "dp"), "seq", "mp"),
        ),
        check_vma=False,
    )
```

```python
import functools
import math

import jax
import jax.numpy as jnp
from jax import lax
from jax.experimental import pallas as pl
from jax.experimental.pallas import tpu as pltpu
from jax.sharding import PartitionSpec as P

DH = 128


highest = lax.Precision.HIGHEST


def entering(value, axis, join, neutral, backward):
    count, mine = (lax.axis_size(axis), lax.axis_index(axis))
    pieces = lax.all_gather(value, axis)
    if backward:
        pieces = pieces[::-1]
        mine = count - 1 - mine
    total = jnp.full_like(value, 0) + jnp.asarray(neutral, value.dtype)

    def hop(position, total):
        longer = join(total, pieces[position])
        return jnp.where(position < mine, longer, total)

    return lax.fori_loop(0, count - 1, hop, total)


def add_states(earlier, later):
    return earlier + later


def per_device(queries, keys, values, grad_output, counts):
    shard_count = lax.axis_size("seq")
    local_rows = queries.shape[1]
    width = queries.shape[2]
    local_heads = width // DH
    capacity = 2 * local_rows // shard_count
    window_rows = shard_count * capacity
    factor = 1.0 / math.sqrt(DH * local_rows * shard_count)
    my_counts = counts[0, 0]
    upto = jnp.arange(shard_count)[:, None] >= jnp.arange(shard_count)[None, :]
    window_ends = jnp.sum(jnp.where(upto, my_counts[None, :], 0), axis=1)
    window_starts = window_ends - my_counts
    offsets = jnp.arange(capacity, dtype=jnp.int32)
    occupied = offsets[None, :] < my_counts[:, None]
    picked = jnp.where(occupied, window_starts[:, None] + offsets[None, :], 0).reshape(-1)
    occupied_column = occupied.reshape(-1, 1)

    def pack(source):
        taken = jnp.take(source[0], picked, axis=0)
        taken = jnp.where(occupied_column, taken, jnp.zeros_like(taken))
        return taken.reshape(shard_count, capacity, width)

    def split_heads(received):
        return received.reshape(window_rows, local_heads, DH)

    def outer_sum(left, right):
        return jnp.einsum("lha,lhb->hab", left, right, preferred_element_type=jnp.float32)

    query_recv, key_recv, value_recv, grad_recv = (
        lax.all_to_all(pack(queries), "seq", split_axis=0, concat_axis=0, tiled=True),
        lax.all_to_all(pack(keys), "seq", split_axis=0, concat_axis=0, tiled=True),
        lax.all_to_all(pack(values), "seq", split_axis=0, concat_axis=0, tiled=True),
        lax.all_to_all(pack(grad_output), "seq", split_axis=0, concat_axis=0, tiled=True),
    )
    query_recv = split_heads(query_recv)
    key_recv = split_heads(key_recv)
    value_recv = split_heads(value_recv)
    grad_recv = split_heads(grad_recv)
    key_state = outer_sum(key_recv, value_recv)
    query_state = outer_sum(query_recv, grad_recv)
    zero_state = jnp.zeros((local_heads, DH, DH), jnp.float32)
    before_kv = entering(key_state, "seq", add_states, zero_state, False)
    after_qd = entering(query_state, "seq", add_states, zero_state, True)
    block = min(512, window_rows)
    nblocks = window_rows // block

    def blocked(received):
        return received.reshape(nblocks, block, local_heads, DH)

    query_blocks = blocked(query_recv)
    key_blocks = blocked(key_recv)
    value_blocks = blocked(value_recv)
    grad_blocks = blocked(grad_recv)
    block_kv = jnp.einsum(
        "nlha,nlhb->nhab", key_blocks, value_blocks, preferred_element_type=jnp.float32
    )
    block_qd = jnp.einsum(
        "nlha,nlhb->nhab", query_blocks, grad_blocks, preferred_element_type=jnp.float32
    )
    kv_before = before_kv[None] + jnp.cumsum(block_kv, axis=0) - block_kv
    qd_after = after_qd[None] + jnp.sum(block_qd, axis=0)[None] - jnp.cumsum(block_qd, axis=0)
    lower = (
        lax.broadcasted_iota(jnp.int32, (block, block), 0)
        >= lax.broadcasted_iota(jnp.int32, (block, block), 1)
    ).astype(jnp.float32)

    def one_block(pieces):
        query_part, key_part, value_part, grad_part, kv_state, qd_state = pieces
        weights = (
            jnp.einsum("rha,sha->hrs", grad_part, value_part, preferred_element_type=jnp.float32)
            * lower[None]
        )
        scores = (
            jnp.einsum("rha,sha->hrs", query_part, key_part, preferred_element_type=jnp.float32)
            * lower[None]
        )
        query_f = query_part.astype(jnp.float32)
        key_f = key_part.astype(jnp.float32)
        value_f = value_part.astype(jnp.float32)
        grad_f = grad_part.astype(jnp.float32)
        grad_q = jnp.einsum("rhb,hab->rha", grad_f, kv_state, precision=highest) + jnp.einsum(
            "hrs,sha->rha", weights, key_f, precision=highest
        )
        grad_k = jnp.einsum("shb,hab->sha", value_f, qd_state, precision=highest) + jnp.einsum(
            "hrs,rha->sha", weights, query_f, precision=highest
        )
        grad_v = jnp.einsum("sha,hab->shb", key_f, qd_state, precision=highest) + jnp.einsum(
            "hrs,rhb->shb", scores, grad_f, precision=highest
        )

        def finish(result):
            return (result * factor).astype(jnp.bfloat16).reshape(block, width)

        return (finish(grad_q), finish(grad_k), finish(grad_v))

    out_q, out_k, out_v = lax.map(
        one_block, (query_blocks, key_blocks, value_blocks, grad_blocks, kv_before, qd_after)
    )

    def to_slots(result):
        return result.reshape(shard_count, capacity, width)

    back_q, back_k, back_v = (
        lax.all_to_all(to_slots(out_q), "seq", split_axis=0, concat_axis=0, tiled=True),
        lax.all_to_all(to_slots(out_k), "seq", split_axis=0, concat_axis=0, tiled=True),
        lax.all_to_all(to_slots(out_v), "seq", split_axis=0, concat_axis=0, tiled=True),
    )
    positions = jnp.arange(local_rows, dtype=jnp.int32)
    member = (
        (positions[:, None] >= window_starts[None, :]) & (positions[:, None] < window_ends[None, :])
    ).astype(jnp.int32)
    window_of = jnp.sum(member * jnp.arange(shard_count, dtype=jnp.int32)[None, :], axis=1)
    start_of = jnp.sum(member * window_starts[None, :], axis=1)
    source_index = window_of * capacity + positions - start_of

    def unpack(returned):
        return jnp.take(returned.reshape(window_rows, width), source_index, axis=0)[None]

    return (unpack(back_q), unpack(back_k), unpack(back_v))


MESH = pl.DeviceIdType.MESH
VMEM_LIMIT = 16 << 20


AHEAD = 4
LAG = 3


def line_kernel(
    rows,
    heads,
    q_ref,
    k_ref,
    v_ref,
    g_ref,
    counts_ref,
    grads_ref,
    qg,
    kv,
    mine,
    ends,
    key_row,
    key_col,
    near,
    grad_out,
    part_out,
    part_in,
    scale_out,
    scale_in,
    mine_sem,
    own_sem,
    ends_send,
    ends_recv,
    qg_send,
    qg_recv,
    kv_send,
    kv_recv,
    pair_send,
    pair_recv,
    dq_send,
    dq_recv,
    part_send,
    part_recv,
    scale_send,
    scale_recv,
):
    n = 4
    me = lax.axis_index("seq")
    factor = 1.0 / math.sqrt(DH * n * rows)
    side = me // 2
    partner = me + 1 - 2 * lax.rem(me, 2)
    opp = n - 1 - me
    cross = n - 1 - partner
    is_inner = jnp.logical_or(me == 1, me == 2)
    is_outer = jnp.logical_not(is_inner)

    def columns(head):
        return pl.ds(pl.multiple_of(head * DH, DH), DH)

    def block(shard):
        return pl.ds(pl.multiple_of(shard * rows, rows), rows)

    def half(shard):
        return block(lax.rem(shard, 2))

    def remote(source, target, send, recv, device):
        return pltpu.make_async_remote_copy(
            src_ref=source,
            dst_ref=target,
            send_sem=send,
            recv_sem=recv,
            device_id={"seq": device},
            device_id_type=MESH,
        )

    barrier = pltpu.get_barrier_semaphore()
    pl.semaphore_signal(barrier, inc=1, device_id={"seq": partner}, device_id_type=MESH)

    @pl.when(is_inner)
    def _():
        pl.semaphore_signal(barrier, inc=1, device_id={"seq": opp}, device_id_type=MESH)

    load = pltpu.make_async_copy(counts_ref, mine, mine_sem)
    load.start()

    def own_copy(h, i):
        source = (g_ref, q_ref, k_ref, v_ref)[i].at[0, :, columns(h)]
        target = qg.at[h, i, block(me)] if i < 2 else kv.at[h, i - 2, half(me)]
        return pltpu.make_async_copy(source, target, own_sem.at[h, i])

    @pl.loop(0, heads)
    def _(h):
        for i in range(4):
            own_copy(h, i).start()

    load.wait()
    lanes = lax.broadcasted_iota(jnp.int32, (8, 128), 1)
    end = jnp.zeros((1, 1), jnp.int32)
    table = jnp.zeros((8, 128), jnp.int32)
    for w in range(n):
        end = end + mine[0, 0:1, w : w + 1]
        table = jnp.where(lanes == w, end, table)
    ends[me] = table

    pl.semaphore_wait(barrier, jnp.where(is_inner, 2, 1))

    def ends_copy(shard, which, device):
        return remote(ends.at[shard], ends.at[shard], ends_send.at[which], ends_recv.at[which], device)

    def qg_copy(h, shard, which, device):
        at = qg.at[h, :, block(shard)]
        return remote(at, at, qg_send.at[h, which], qg_recv.at[h, which], device)

    def group_copy(h, shard):
        at = qg.at[pl.ds(h, 4), :, block(shard)]
        return remote(at, at, qg_send.at[h, 1], qg_recv.at[h, 1], opp)

    def kv_copy(h, shard):
        at = kv.at[h, :, half(shard)]
        return remote(at, at, kv_send.at[h], kv_recv.at[h], partner)

    @pl.when(is_outer)
    def _():
        ends_copy(me, 0, partner).start()

        def give_qg(h):
            own_copy(h, 0).wait()
            own_copy(h, 1).wait()
            qg_copy(h, me, 0, partner).start()

        def give_kv(h):
            own_copy(h, 2).wait()
            own_copy(h, 3).wait()
            kv_copy(h, me).start()

        give_qg(0)

        @pl.loop(0, heads)
        def _(h):
            give_kv(h)
            for later in (2 * h + 1, 2 * h + 2):

                @pl.when(later < heads)
                def _():
                    give_qg(later)

    def scores(left, right):
        return lax.dot_general(
            left, right, (((1,), (1,)), ((), ())), preferred_element_type=jnp.float32
        )

    def weighted(weights, right):
        high = weights.astype(jnp.bfloat16)
        low = (weights - high.astype(jnp.float32)).astype(jnp.bfloat16)
        product = jnp.dot(high, right, preferred_element_type=jnp.float32) + jnp.dot(
            low, right, preferred_element_type=jnp.float32
        )
        return product * factor

    def masked(weights, at, others, forward):
        col = key_col[pl.ds(2 * at, 2)].reshape(2 * rows, 128)
        pieces = []
        for i, other in enumerate(others):
            row = key_row[other][0:1, :]
            keep = (row <= col) if forward else (row >= col)
            pieces.append(jnp.where(keep, weights[:, i * rows : (i + 1) * rows], 0.0))
        return jnp.concatenate(pieces, axis=1)

    def part_copy(h, which):
        return remote(
            part_out.at[h, which],
            part_in.at[h, which],
            part_send.at[h, which],
            part_recv.at[h, which],
            opp,
        )

    def scale_copy(h):
        return remote(scale_out.at[h], scale_in.at[h], scale_send.at[h], scale_recv.at[h], opp)

    def pair_copy(h, which):
        source, target = grad_out.at[h, which, pl.ds(1, 2)], grads_ref.at[pl.ds(1, 2), :, columns(h)]
        if which == 1:
            return pltpu.make_async_copy(source, target, pair_send.at[h, 1])
        return remote(source, target, pair_send.at[h, 0], pair_recv.at[h], partner)

    def dq_copy(h, which):
        source, target = grad_out.at[h, which, 0], grads_ref.at[0, :, columns(h)]
        if which == 1:
            return pltpu.make_async_copy(source, target, dq_send.at[h, 1])
        return remote(source, target, dq_send.at[h, 0], dq_recv.at[h], partner)

    @pl.when(is_inner)
    def _():
        ends_copy(me, 1, opp).start()

        def group_to_opp(first):
            @pl.loop(first, first + 4)
            def _(h):
                own_copy(h, 0).wait()
                own_copy(h, 1).wait()

            group_copy(first, me).start()

        group_to_opp(0)

        ends_copy(partner, 0, partner).wait_recv()
        ends_copy(partner, 2, opp).start()

        def relay(h):
            qg_copy(h, partner, 0, partner).wait_recv()
            qg_copy(h, partner, 2, opp).start()

        relay(0)

        for first in range(4, heads, 4):
            group_to_opp(first)

        ends_copy(opp, 1, opp).wait_recv()
        ends_copy(cross, 2, opp).wait_recv()

        across = lax.broadcasted_iota(jnp.int32, (8, rows), 1)
        down = lax.broadcasted_iota(jnp.int32, (rows, 128), 0)
        for s in range(n):
            window_row = jnp.zeros((8, rows), jnp.int32)
            window_col = jnp.zeros((rows, 128), jnp.int32)
            for w in range(n):
                stop = ends[s, 0:1, w : w + 1]
                window_row = window_row + jnp.where(across >= stop, 1, 0)
                window_col = window_col + jnp.where(down >= stop, 1, 0)
            key_row[s] = (window_row * n + s) * rows + across
            key_col[s] = (window_col * n + s) * rows + down

        def finish(h, which):
            part_copy(h, which).wait_recv()
            far = part_in[h, which].astype(jnp.int32).astype(jnp.float32) * scale_in[h, which]
            grad_out[h, which, 0] = (near[h, which] + far).astype(jnp.bfloat16)
            dq_copy(h, which).start()

        def finish_outer(h):
            scale_copy(h).wait_recv()
            finish(h, 0)

        @pl.loop(0, heads)
        def _(h):
            for later in (2 * h + 1, 2 * h + 2):

                @pl.when(later < heads)
                def _():
                    relay(later)

            own_copy(h, 2).wait()
            own_copy(h, 3).wait()
            kv_copy(h, partner).wait_recv()
            key_all = kv[h, 0]
            value_all = kv[h, 1]
            def part(at):
                grad = qg[h, 0, pl.ds(pl.multiple_of(2 * at * rows, 2 * rows), 2 * rows), :]
                weights = masked(scores(grad, value_all), at, (2 * side, 2 * side + 1), True)
                return weighted(weights, key_all)

            @pl.when(lax.rem(h, 4) == 0)
            def _():
                group_copy(h, opp).wait_recv()

            qg_copy(h, cross, 2, opp).wait_recv()
            both = part(1 - side)
            for i in range(2):
                which = (1 - side) if i == 0 else side
                far = both[i * rows : (i + 1) * rows]
                top = jnp.maximum(jnp.max(jnp.abs(far), axis=0, keepdims=True), 1e-30)
                part_out[h, which] = jnp.round(far * (32767.0 / top)).astype(jnp.int32).astype(jnp.int16)
                scale_out[h, which] = top * (1.0 / 32767.0)
            part_copy(h, 0).start()
            scale_copy(h).start()

            @pl.when(h >= 6)
            def _():
                part_copy(h - 6, 1).start()

            both = part(side)
            for i in range(2):
                near[h, side if i == 0 else 1 - side] = both[i * rows : (i + 1) * rows]
            grad_all = qg[h, 0]
            query_all = qg[h, 1]
            shards = tuple(range(n))
            for j, left, over, right in (
                (1, value_all, grad_all, query_all),
                (2, key_all, query_all, grad_all),
            ):
                both = weighted(masked(scores(left, over), side, shards, False), right)
                for i in range(2):
                    which = side if i == 0 else 1 - side
                    grad_out[h, which, j] = both[i * rows : (i + 1) * rows].astype(jnp.bfloat16)
            for which in range(2):
                pair_copy(h, which).start()

            @pl.when(h == heads - 1)
            def _():
                @pl.loop(heads - 6, heads)
                def _(held):
                    part_copy(held, 1).start()

            @pl.when(h >= LAG)
            def _():
                finish_outer(h - LAG)

        @pl.loop(heads - LAG, heads)
        def _(h):
            finish_outer(h)

        @pl.loop(0, heads)
        def _(h):
            finish(h, 1)

        ends_copy(me, 1, opp).wait_send()
        ends_copy(partner, 2, opp).wait_send()

        @pl.loop(0, heads)
        def _(h):
            @pl.when(lax.rem(h, 4) == 0)
            def _():
                group_copy(h, me).wait_send()

            qg_copy(h, partner, 2, opp).wait_send()
            pair_copy(h, 0).wait_send()
            pair_copy(h, 1).wait()
            part_copy(h, 0).wait_send()
            part_copy(h, 1).wait_send()
            scale_copy(h).wait_send()
            dq_copy(h, 0).wait_send()
            dq_copy(h, 1).wait()

    @pl.when(is_outer)
    def _():
        ends_copy(me, 0, partner).wait_send()

        @pl.loop(0, heads)
        def _(h):
            qg_copy(h, me, 0, partner).wait_send()
            kv_copy(h, me).wait_send()
            pair_copy(h, 0).wait_recv()
            dq_copy(h, 0).wait_recv()


def place_kernel(grads_ref, dq_ref, dk_ref, dv_ref, sem):
    copies = [
        pltpu.make_async_copy(grads_ref.at[i], target.at[0], sem.at[i])
        for i, target in enumerate((dq_ref, dk_ref, dv_ref))
    ]
    for copy in copies:
        copy.start()
    for copy in copies:
        copy.wait()


def by_line(queries, keys, values, grad_output, counts):
    n = 4
    rows, width = queries.shape[1:]
    heads = width // DH
    dma = pltpu.SemaphoreType.DMA
    anywhere = pl.BlockSpec(memory_space=pl.ANY)
    packed = pl.pallas_call(
        functools.partial(line_kernel, rows, heads),
        out_shape=jax.ShapeDtypeStruct((3, rows, width), jnp.bfloat16),
        in_specs=[pl.BlockSpec(memory_space=pltpu.HBM)] * 5,
        out_specs=anywhere,
        scratch_shapes=[
            pltpu.VMEM((heads, 2, n * rows, DH), jnp.bfloat16),
            pltpu.VMEM((heads, 2, 2 * rows, DH), jnp.bfloat16),
            pltpu.VMEM((1, 1, n), jnp.int32),
            pltpu.VMEM((n, 8, 128), jnp.int32),
            pltpu.VMEM((n, 8, rows), jnp.int32),
            pltpu.VMEM((n, rows, 128), jnp.int32),
            pltpu.VMEM((heads, 2, rows, DH), jnp.float32),
            pltpu.VMEM((heads, 2, 3, rows, DH), jnp.bfloat16),
            pltpu.VMEM((heads, 2, rows, DH), jnp.int16),
            pltpu.VMEM((heads, 2, rows, DH), jnp.int16),
            pltpu.VMEM((heads, 2, 1, DH), jnp.float32),
            pltpu.VMEM((heads, 2, 1, DH), jnp.float32),
            dma(()),
            dma((heads, 4)),
            dma((3,)),
            dma((3,)),
            dma((heads, 3)),
            dma((heads, 3)),
            dma((heads,)),
            dma((heads,)),
            dma((heads, 2)),
            dma((heads,)),
            dma((heads, 2)),
            dma((heads,)),
            dma((heads, 2)),
            dma((heads, 2)),
            dma((heads,)),
            dma((heads,)),
        ],
        compiler_params=pltpu.CompilerParams(collective_id=0, has_side_effects=True, vmem_limit_bytes=VMEM_LIMIT),
    )(*(pltpu.with_memory_space_constraint(x, pltpu.HBM) for x in (queries, keys, values, grad_output, counts)))
    return pl.pallas_call(
        place_kernel,
        out_shape=[jax.ShapeDtypeStruct(queries.shape, jnp.bfloat16)] * 3,
        in_specs=[anywhere],
        out_specs=[anywhere] * 3,
        scratch_shapes=[dma((3,))],
        compiler_params=pltpu.CompilerParams(vmem_limit_bytes=VMEM_LIMIT),
    )(packed)


def per_shard(queries, keys, values, grad_output, counts):
    n = lax.axis_size("seq")
    if n == 4 and queries.shape[1] == 128:
        return by_line(queries, keys, values, grad_output, counts)
    return per_device(queries, keys, values, grad_output, counts)


def solution(mesh):
    placed = (
        P(("groups", "dp"), "seq", "mp"),
        P(("groups", "dp"), "seq", "mp"),
        P(("groups", "dp"), "seq", "mp"),
        P(("groups", "dp"), "seq", "mp"),
        P(("groups", "dp"), "seq", None),
    )
    return jax.shard_map(
        per_shard,
        mesh=mesh,
        in_specs=placed,
        out_specs=(
            P(("groups", "dp"), "seq", "mp"),
            P(("groups", "dp"), "seq", "mp"),
            P(("groups", "dp"), "seq", "mp"),
        ),
        check_vma=False,
    )
```

```python
import functools
import math

import jax
import jax.numpy as jnp
from jax import lax
from jax.experimental import pallas as pl
from jax.experimental.pallas import tpu as pltpu
from jax.sharding import PartitionSpec as P

DH = 128


highest = lax.Precision.HIGHEST


def entering(value, axis, join, neutral, backward):
    count, mine = (lax.axis_size(axis), lax.axis_index(axis))
    pieces = lax.all_gather(value, axis)
    if backward:
        pieces = pieces[::-1]
        mine = count - 1 - mine
    total = jnp.full_like(value, 0) + jnp.asarray(neutral, value.dtype)

    def hop(position, total):
        longer = join(total, pieces[position])
        return jnp.where(position < mine, longer, total)

    return lax.fori_loop(0, count - 1, hop, total)


def add_states(earlier, later):
    return earlier + later


def per_device(queries, keys, values, grad_output, counts):
    shard_count = lax.axis_size("seq")
    local_rows = queries.shape[1]
    width = queries.shape[2]
    local_heads = width // DH
    capacity = 2 * local_rows // shard_count
    window_rows = shard_count * capacity
    factor = 1.0 / math.sqrt(DH * local_rows * shard_count)
    my_counts = counts[0, 0]
    upto = jnp.arange(shard_count)[:, None] >= jnp.arange(shard_count)[None, :]
    window_ends = jnp.sum(jnp.where(upto, my_counts[None, :], 0), axis=1)
    window_starts = window_ends - my_counts
    offsets = jnp.arange(capacity, dtype=jnp.int32)
    occupied = offsets[None, :] < my_counts[:, None]
    picked = jnp.where(occupied, window_starts[:, None] + offsets[None, :], 0).reshape(-1)
    occupied_column = occupied.reshape(-1, 1)

    def pack(source):
        taken = jnp.take(source[0], picked, axis=0)
        taken = jnp.where(occupied_column, taken, jnp.zeros_like(taken))
        return taken.reshape(shard_count, capacity, width)

    def split_heads(received):
        return received.reshape(window_rows, local_heads, DH)

    def outer_sum(left, right):
        return jnp.einsum("lha,lhb->hab", left, right, preferred_element_type=jnp.float32)

    query_recv, key_recv, value_recv, grad_recv = (
        lax.all_to_all(pack(queries), "seq", split_axis=0, concat_axis=0, tiled=True),
        lax.all_to_all(pack(keys), "seq", split_axis=0, concat_axis=0, tiled=True),
        lax.all_to_all(pack(values), "seq", split_axis=0, concat_axis=0, tiled=True),
        lax.all_to_all(pack(grad_output), "seq", split_axis=0, concat_axis=0, tiled=True),
    )
    query_recv = split_heads(query_recv)
    key_recv = split_heads(key_recv)
    value_recv = split_heads(value_recv)
    grad_recv = split_heads(grad_recv)
    key_state = outer_sum(key_recv, value_recv)
    query_state = outer_sum(query_recv, grad_recv)
    zero_state = jnp.zeros((local_heads, DH, DH), jnp.float32)
    before_kv = entering(key_state, "seq", add_states, zero_state, False)
    after_qd = entering(query_state, "seq", add_states, zero_state, True)
    block = min(512, window_rows)
    nblocks = window_rows // block

    def blocked(received):
        return received.reshape(nblocks, block, local_heads, DH)

    query_blocks = blocked(query_recv)
    key_blocks = blocked(key_recv)
    value_blocks = blocked(value_recv)
    grad_blocks = blocked(grad_recv)
    block_kv = jnp.einsum(
        "nlha,nlhb->nhab", key_blocks, value_blocks, preferred_element_type=jnp.float32
    )
    block_qd = jnp.einsum(
        "nlha,nlhb->nhab", query_blocks, grad_blocks, preferred_element_type=jnp.float32
    )
    kv_before = before_kv[None] + jnp.cumsum(block_kv, axis=0) - block_kv
    qd_after = after_qd[None] + jnp.sum(block_qd, axis=0)[None] - jnp.cumsum(block_qd, axis=0)
    lower = (
        lax.broadcasted_iota(jnp.int32, (block, block), 0)
        >= lax.broadcasted_iota(jnp.int32, (block, block), 1)
    ).astype(jnp.float32)

    def one_block(pieces):
        query_part, key_part, value_part, grad_part, kv_state, qd_state = pieces
        weights = (
            jnp.einsum("rha,sha->hrs", grad_part, value_part, preferred_element_type=jnp.float32)
            * lower[None]
        )
        scores = (
            jnp.einsum("rha,sha->hrs", query_part, key_part, preferred_element_type=jnp.float32)
            * lower[None]
        )
        query_f = query_part.astype(jnp.float32)
        key_f = key_part.astype(jnp.float32)
        value_f = value_part.astype(jnp.float32)
        grad_f = grad_part.astype(jnp.float32)
        grad_q = jnp.einsum("rhb,hab->rha", grad_f, kv_state, precision=highest) + jnp.einsum(
            "hrs,sha->rha", weights, key_f, precision=highest
        )
        grad_k = jnp.einsum("shb,hab->sha", value_f, qd_state, precision=highest) + jnp.einsum(
            "hrs,rha->sha", weights, query_f, precision=highest
        )
        grad_v = jnp.einsum("sha,hab->shb", key_f, qd_state, precision=highest) + jnp.einsum(
            "hrs,rhb->shb", scores, grad_f, precision=highest
        )

        def finish(result):
            return (result * factor).astype(jnp.bfloat16).reshape(block, width)

        return (finish(grad_q), finish(grad_k), finish(grad_v))

    out_q, out_k, out_v = lax.map(
        one_block, (query_blocks, key_blocks, value_blocks, grad_blocks, kv_before, qd_after)
    )

    def to_slots(result):
        return result.reshape(shard_count, capacity, width)

    back_q, back_k, back_v = (
        lax.all_to_all(to_slots(out_q), "seq", split_axis=0, concat_axis=0, tiled=True),
        lax.all_to_all(to_slots(out_k), "seq", split_axis=0, concat_axis=0, tiled=True),
        lax.all_to_all(to_slots(out_v), "seq", split_axis=0, concat_axis=0, tiled=True),
    )
    positions = jnp.arange(local_rows, dtype=jnp.int32)
    member = (
        (positions[:, None] >= window_starts[None, :]) & (positions[:, None] < window_ends[None, :])
    ).astype(jnp.int32)
    window_of = jnp.sum(member * jnp.arange(shard_count, dtype=jnp.int32)[None, :], axis=1)
    start_of = jnp.sum(member * window_starts[None, :], axis=1)
    source_index = window_of * capacity + positions - start_of

    def unpack(returned):
        return jnp.take(returned.reshape(window_rows, width), source_index, axis=0)[None]

    return (unpack(back_q), unpack(back_k), unpack(back_v))


MESH = pl.DeviceIdType.MESH
VMEM_LIMIT = 16 << 20


AHEAD = 4
LAG = 3


def line_kernel(
    rows,
    heads,
    q_ref,
    k_ref,
    v_ref,
    g_ref,
    counts_ref,
    grads_ref,
    qg,
    kv,
    mine,
    ends,
    key_row,
    key_col,
    near,
    grad_out,
    part_out,
    part_in,
    scale_out,
    scale_in,
    mine_sem,
    own_sem,
    ends_send,
    ends_recv,
    qg_send,
    qg_recv,
    kv_send,
    kv_recv,
    pair_send,
    pair_recv,
    dq_send,
    dq_recv,
    part_send,
    part_recv,
    scale_send,
    scale_recv,
):
    n = 4
    me = lax.axis_index("seq")
    factor = 1.0 / math.sqrt(DH * n * rows)
    side = me // 2
    partner = me + 1 - 2 * lax.rem(me, 2)
    opp = n - 1 - me
    cross = n - 1 - partner
    is_inner = jnp.logical_or(me == 1, me == 2)
    is_outer = jnp.logical_not(is_inner)

    def columns(head):
        return pl.ds(pl.multiple_of(head * DH, DH), DH)

    def block(shard):
        return pl.ds(pl.multiple_of(shard * rows, rows), rows)

    def half(shard):
        return block(lax.rem(shard, 2))

    def remote(source, target, send, recv, device):
        return pltpu.make_async_remote_copy(
            src_ref=source,
            dst_ref=target,
            send_sem=send,
            recv_sem=recv,
            device_id={"seq": device},
            device_id_type=MESH,
        )

    barrier = pltpu.get_barrier_semaphore()
    pl.semaphore_signal(barrier, inc=1, device_id={"seq": partner}, device_id_type=MESH)

    @pl.when(is_inner)
    def _():
        pl.semaphore_signal(barrier, inc=1, device_id={"seq": opp}, device_id_type=MESH)

    load = pltpu.make_async_copy(counts_ref, mine, mine_sem)
    load.start()

    def own_copy(h, i):
        source = (g_ref, q_ref, k_ref, v_ref)[i].at[0, :, columns(h)]
        target = qg.at[h, i, block(me)] if i < 2 else kv.at[h, i - 2, half(me)]
        return pltpu.make_async_copy(source, target, own_sem.at[h, i])

    @pl.loop(0, heads)
    def _(h):
        for i in range(4):
            own_copy(h, i).start()

    load.wait()
    lanes = lax.broadcasted_iota(jnp.int32, (8, 128), 1)
    end = jnp.zeros((1, 1), jnp.int32)
    table = jnp.zeros((8, 128), jnp.int32)
    for w in range(n):
        end = end + mine[0, 0:1, w : w + 1]
        table = jnp.where(lanes == w, end, table)
    ends[me] = table

    pl.semaphore_wait(barrier, jnp.where(is_inner, 2, 1))

    def ends_copy(shard, which, device):
        return remote(ends.at[shard], ends.at[shard], ends_send.at[which], ends_recv.at[which], device)

    def qg_copy(h, shard, which, device):
        at = qg.at[h, :, block(shard)]
        return remote(at, at, qg_send.at[h, which], qg_recv.at[h, which], device)

    def group_copy(h, shard):
        at = qg.at[pl.ds(h, 4), :, block(shard)]
        return remote(at, at, qg_send.at[h, 1], qg_recv.at[h, 1], opp)

    def kv_copy(h, shard):
        at = kv.at[h, :, half(shard)]
        return remote(at, at, kv_send.at[h], kv_recv.at[h], partner)

    @pl.when(is_outer)
    def _():
        ends_copy(me, 0, partner).start()

        def give_qg(h):
            own_copy(h, 0).wait()
            own_copy(h, 1).wait()
            qg_copy(h, me, 0, partner).start()

        def give_kv(h):
            own_copy(h, 2).wait()
            own_copy(h, 3).wait()
            kv_copy(h, me).start()

        give_qg(0)

        @pl.loop(0, heads)
        def _(h):
            give_kv(h)
            for later in (2 * h + 1, 2 * h + 2):

                @pl.when(later < heads)
                def _():
                    give_qg(later)

    def scores(left, right):
        return lax.dot_general(
            left, right, (((1,), (1,)), ((), ())), preferred_element_type=jnp.float32
        )

    def weighted(weights, right):
        high = weights.astype(jnp.bfloat16)
        low = (weights - high.astype(jnp.float32)).astype(jnp.bfloat16)
        product = jnp.dot(high, right, preferred_element_type=jnp.float32) + jnp.dot(
            low, right, preferred_element_type=jnp.float32
        )
        return product * factor

    def masked(weights, at, others, forward):
        col = key_col[pl.ds(2 * at, 2)].reshape(2 * rows, 128)
        pieces = []
        for i, other in enumerate(others):
            row = key_row[other][0:1, :]
            keep = (row <= col) if forward else (row >= col)
            pieces.append(jnp.where(keep, weights[:, i * rows : (i + 1) * rows], 0.0))
        return jnp.concatenate(pieces, axis=1)

    def part_copy(h, which):
        return remote(
            part_out.at[h, which],
            part_in.at[h, which],
            part_send.at[h, which],
            part_recv.at[h, which],
            opp,
        )

    def scale_copy(h):
        return remote(scale_out.at[h], scale_in.at[h], scale_send.at[h], scale_recv.at[h], opp)

    def pair_copy(h, which):
        source, target = grad_out.at[h, which, pl.ds(1, 2)], grads_ref.at[pl.ds(1, 2), :, columns(h)]
        if which == 1:
            return pltpu.make_async_copy(source, target, pair_send.at[h, 1])
        return remote(source, target, pair_send.at[h, 0], pair_recv.at[h], partner)

    def dq_copy(h, which):
        source, target = grad_out.at[h, which, 0], grads_ref.at[0, :, columns(h)]
        if which == 1:
            return pltpu.make_async_copy(source, target, dq_send.at[h, 1])
        return remote(source, target, dq_send.at[h, 0], dq_recv.at[h], partner)

    @pl.when(is_inner)
    def _():
        ends_copy(me, 1, opp).start()

        def group_to_opp(first):
            @pl.loop(first, first + 4)
            def _(h):
                own_copy(h, 0).wait()
                own_copy(h, 1).wait()

            group_copy(first, me).start()

        group_to_opp(0)

        ends_copy(partner, 0, partner).wait_recv()
        ends_copy(partner, 2, opp).start()

        def relay(h):
            qg_copy(h, partner, 0, partner).wait_recv()
            qg_copy(h, partner, 2, opp).start()

        relay(0)

        for first in range(4, heads, 4):
            group_to_opp(first)

        ends_copy(opp, 1, opp).wait_recv()
        ends_copy(cross, 2, opp).wait_recv()

        across = lax.broadcasted_iota(jnp.int32, (8, rows), 1)
        down = lax.broadcasted_iota(jnp.int32, (rows, 128), 0)
        for s in range(n):
            window_row = jnp.zeros((8, rows), jnp.int32)
            window_col = jnp.zeros((rows, 128), jnp.int32)
            for w in range(n):
                stop = ends[s, 0:1, w : w + 1]
                window_row = window_row + jnp.where(across >= stop, 1, 0)
                window_col = window_col + jnp.where(down >= stop, 1, 0)
            key_row[s] = (window_row * n + s) * rows + across
            key_col[s] = (window_col * n + s) * rows + down

        def finish(h, which):
            part_copy(h, which).wait_recv()
            far = part_in[h, which].astype(jnp.int32).astype(jnp.float32) * scale_in[h, which]
            grad_out[h, which, 0] = (near[h, which] + far).astype(jnp.bfloat16)
            dq_copy(h, which).start()

        def finish_outer(h):
            scale_copy(h).wait_recv()
            finish(h, 0)

        @pl.loop(0, heads)
        def _(h):
            for later in (2 * h + 1, 2 * h + 2):

                @pl.when(later < heads)
                def _():
                    relay(later)

            own_copy(h, 2).wait()
            own_copy(h, 3).wait()
            kv_copy(h, partner).wait_recv()
            key_all = kv[h, 0]
            value_all = kv[h, 1]
            def part(at):
                grad = qg[h, 0, pl.ds(pl.multiple_of(2 * at * rows, 2 * rows), 2 * rows), :]
                weights = masked(scores(grad, value_all), at, (2 * side, 2 * side + 1), True)
                return weighted(weights, key_all)

            @pl.when(lax.rem(h, 4) == 0)
            def _():
                group_copy(h, opp).wait_recv()

            qg_copy(h, cross, 2, opp).wait_recv()
            both = part(1 - side)
            for i in range(2):
                which = (1 - side) if i == 0 else side
                far = both[i * rows : (i + 1) * rows]
                top = jnp.maximum(jnp.max(jnp.abs(far), axis=0, keepdims=True), 1e-30)
                part_out[h, which] = jnp.round(far * (32767.0 / top)).astype(jnp.int32).astype(jnp.int16)
                scale_out[h, which] = top * (1.0 / 32767.0)
            part_copy(h, 0).start()
            scale_copy(h).start()

            @pl.when(h >= 6)
            def _():
                part_copy(h - 6, 1).start()

            grad_all = qg[h, 0]
            query_all = qg[h, 1]
            shards = tuple(range(n))
            for j, left, over, right in (
                (1, value_all, grad_all, query_all),
                (2, key_all, query_all, grad_all),
            ):
                both = weighted(masked(scores(left, over), side, shards, False), right)
                for i in range(2):
                    which = side if i == 0 else 1 - side
                    grad_out[h, which, j] = both[i * rows : (i + 1) * rows].astype(jnp.bfloat16)
            for which in range(2):
                pair_copy(h, which).start()

            both = part(side)
            for i in range(2):
                near[h, side if i == 0 else 1 - side] = both[i * rows : (i + 1) * rows]

            @pl.when(h == heads - 1)
            def _():
                @pl.loop(heads - 6, heads)
                def _(held):
                    part_copy(held, 1).start()

            @pl.when(h >= LAG)
            def _():
                finish_outer(h - LAG)

        @pl.loop(heads - LAG, heads)
        def _(h):
            finish_outer(h)

        @pl.loop(0, heads)
        def _(h):
            finish(h, 1)

        ends_copy(me, 1, opp).wait_send()
        ends_copy(partner, 2, opp).wait_send()

        @pl.loop(0, heads)
        def _(h):
            @pl.when(lax.rem(h, 4) == 0)
            def _():
                group_copy(h, me).wait_send()

            qg_copy(h, partner, 2, opp).wait_send()
            pair_copy(h, 0).wait_send()
            pair_copy(h, 1).wait()
            part_copy(h, 0).wait_send()
            part_copy(h, 1).wait_send()
            scale_copy(h).wait_send()
            dq_copy(h, 0).wait_send()
            dq_copy(h, 1).wait()

    @pl.when(is_outer)
    def _():
        ends_copy(me, 0, partner).wait_send()

        @pl.loop(0, heads)
        def _(h):
            qg_copy(h, me, 0, partner).wait_send()
            kv_copy(h, me).wait_send()
            pair_copy(h, 0).wait_recv()
            dq_copy(h, 0).wait_recv()


def place_kernel(grads_ref, dq_ref, dk_ref, dv_ref, sem):
    copies = [
        pltpu.make_async_copy(grads_ref.at[i], target.at[0], sem.at[i])
        for i, target in enumerate((dq_ref, dk_ref, dv_ref))
    ]
    for copy in copies:
        copy.start()
    for copy in copies:
        copy.wait()


def by_line(queries, keys, values, grad_output, counts):
    n = 4
    rows, width = queries.shape[1:]
    heads = width // DH
    dma = pltpu.SemaphoreType.DMA
    anywhere = pl.BlockSpec(memory_space=pl.ANY)
    packed = pl.pallas_call(
        functools.partial(line_kernel, rows, heads),
        out_shape=jax.ShapeDtypeStruct((3, rows, width), jnp.bfloat16),
        in_specs=[pl.BlockSpec(memory_space=pltpu.HBM)] * 5,
        out_specs=anywhere,
        scratch_shapes=[
            pltpu.VMEM((heads, 2, n * rows, DH), jnp.bfloat16),
            pltpu.VMEM((heads, 2, 2 * rows, DH), jnp.bfloat16),
            pltpu.VMEM((1, 1, n), jnp.int32),
            pltpu.VMEM((n, 8, 128), jnp.int32),
            pltpu.VMEM((n, 8, rows), jnp.int32),
            pltpu.VMEM((n, rows, 128), jnp.int32),
            pltpu.VMEM((heads, 2, rows, DH), jnp.float32),
            pltpu.VMEM((heads, 2, 3, rows, DH), jnp.bfloat16),
            pltpu.VMEM((heads, 2, rows, DH), jnp.int16),
            pltpu.VMEM((heads, 2, rows, DH), jnp.int16),
            pltpu.VMEM((heads, 2, 1, DH), jnp.float32),
            pltpu.VMEM((heads, 2, 1, DH), jnp.float32),
            dma(()),
            dma((heads, 4)),
            dma((3,)),
            dma((3,)),
            dma((heads, 3)),
            dma((heads, 3)),
            dma((heads,)),
            dma((heads,)),
            dma((heads, 2)),
            dma((heads,)),
            dma((heads, 2)),
            dma((heads,)),
            dma((heads, 2)),
            dma((heads, 2)),
            dma((heads,)),
            dma((heads,)),
        ],
        compiler_params=pltpu.CompilerParams(collective_id=0, has_side_effects=True, vmem_limit_bytes=VMEM_LIMIT),
    )(*(pltpu.with_memory_space_constraint(x, pltpu.HBM) for x in (queries, keys, values, grad_output, counts)))
    return pl.pallas_call(
        place_kernel,
        out_shape=[jax.ShapeDtypeStruct(queries.shape, jnp.bfloat16)] * 3,
        in_specs=[anywhere],
        out_specs=[anywhere] * 3,
        scratch_shapes=[dma((3,))],
        compiler_params=pltpu.CompilerParams(vmem_limit_bytes=VMEM_LIMIT),
    )(packed)


def per_shard(queries, keys, values, grad_output, counts):
    n = lax.axis_size("seq")
    if n == 4 and queries.shape[1] == 128:
        return by_line(queries, keys, values, grad_output, counts)
    return per_device(queries, keys, values, grad_output, counts)


def solution(mesh):
    placed = (
        P(("groups", "dp"), "seq", "mp"),
        P(("groups", "dp"), "seq", "mp"),
        P(("groups", "dp"), "seq", "mp"),
        P(("groups", "dp"), "seq", "mp"),
        P(("groups", "dp"), "seq", None),
    )
    return jax.shard_map(
        per_shard,
        mesh=mesh,
        in_specs=placed,
        out_specs=(
            P(("groups", "dp"), "seq", "mp"),
            P(("groups", "dp"), "seq", "mp"),
            P(("groups", "dp"), "seq", "mp"),
        ),
        check_vma=False,
    )
```
